32 devices in a mesh: row: 4 (over y, core), col: 8 (over z, x).
Axes of the slice: x: 2, y: 2, z: 4, core: 2. Of those that a mesh axis runs over, the one named last changes fastest.
Arguments:
- points: bfloat16 [65536, 512], P(('row', 'col')), may hold values from -6 to 6
- factor: bfloat16 [65536, 2048], P(('row', 'col')), may hold values from -0.078125 to 0.078125
- targets: bfloat16 [65536, 256], P(('row', 'col')), may hold values from -6 to 6
- pivot_slots: int32 [32, 32], P(('row', 'col')), may hold values from 0 to 2047, as said below
- pivot_counts: int32 [32], replicated, may hold values from 1 to 32, 512 in all
Outputs:
- new_columns: bfloat16 [512, 65536], P(None, ('row', 'col'))
- residual_next: float32 [65536, 256], P(('row', 'col'))
The draws below stay inside these ranges and needn't reach their ends.
Inputs may be any that keep to these rules, and one draw needn't show every extreme that they name: `pivot_slots`: each row holds 32 different local row numbers; row d's first pivot_counts[d] entries are device d's pivots, the rest are unused. `pivot_counts`: the counts sum to 512; one of them is 32.
All inputs are finite; a program needn't handle non-finite values.
Results may differ from the reference program's by a relative error of at most 0.0029.
Values may be sent and summed in bfloat16 or wider, within the bound.
No kernel may reach another device: no remote copies, remote signals or barrier semaphores. Data moves between devices by JAX's collectives and lax.ppermute only.
A program may use at most 128 MiB of HBM per device.

```python
import math
import jax
import jax.numpy as jnp
import numpy as np
from jax import lax

D = 512
K_HELD = 2048
BLOCK = 512
NT = 256
PTS_DEV = 2048
CAP = 32
NPTS = 65536
DEVICES = 32


def draw_pivot_slots(key, part):
    device_keys = jax.random.split(jax.random.fold_in(key, 17), DEVICES)

    def device_draw(device_key):
        return jax.random.permutation(device_key, PTS_DEV)[:CAP]
    return jax.vmap(device_draw)(device_keys).astype(jnp.int32)


def spiked(array, own_key, source, target, parts, factor):
    def block_of(axis_at):
        return (jnp.arange(array.shape[axis_at]) // (array.shape[axis_at] // parts)).reshape((-1,) + (1,) * (array.ndim - 1 - axis_at))

    near = jax.random.permutation(own_key, parts)[block_of(target)]
    far = (block_of(target) + parts // 2) % parts
    return jnp.where((block_of(source) == near) | (block_of(source) == far), factor * array, array)


def level_of(rng, dims, pieces, low, high):
    gain = 1.0
    for dim, parts in pieces:
        steps = jax.random.uniform(jax.random.fold_in(jax.random.fold_in(rng, 6), dim), (parts,), jnp.float32, low / len(pieces), high / len(pieces))
        gain = gain * jnp.repeat(jnp.exp(steps), dims[dim] // parts).reshape((-1,) + (1,) * (len(dims) - 1 - dim))
    return gain


def profile(number_of, total, limit, skew):
    portions = [(1 << 20) // math.isqrt(grade ** skew) + 1 for grade in range(2, number_of + 1)]
    surplus, counts = total - limit - (number_of - 1), [1] * (number_of - 1)
    while surplus > 0:
        free = [i for i in range(number_of - 1) if counts[i] < limit]
        whole, remaining = sum([portions[i] for i in free]), surplus
        for i in free:
            addition = min(limit - counts[i], max(1, remaining * portions[i] // whole), surplus)
            counts[i] = counts[i] + addition
            surplus = surplus - addition
    return np.array([limit] + counts)


def ragged(own_key, number_of, total, reach, skew):
    if number_of == 2:
        one = jax.random.randint(own_key, (), max(1, total - reach), min(reach, total - 1) + 1)
        return jnp.stack([one, total - one])
    sizes = jnp.asarray(profile(number_of, total, reach, skew), jnp.int32)
    pairs = (number_of - 1) // 2
    giver, receiver = sizes[1:1 + 2 * pairs:2], sizes[2:2 + 2 * pairs:2]
    slack = jnp.minimum(giver - 1, reach - receiver)
    passed = jax.random.randint(jax.random.fold_in(own_key, 1), (pairs,), 0, 1 << 20) % (slack + 1)
    sizes = sizes.at[1:1 + 2 * pairs:2].set(giver - passed).at[2:2 + 2 * pairs:2].set(receiver + passed)
    return sizes[jax.random.permutation(jax.random.fold_in(own_key, 2), number_of)]


def gaussian(stream_key, extent, deviation, bound, cuts=(), held_as=jnp.bfloat16):
    result = jax.random.normal(stream_key, extent, jnp.float32) * deviation
    if len(cuts) > 0:
        result = level_of(stream_key, extent, cuts, -0.22, 0.18) * result
    return jnp.clip(result, min=-bound, max=bound).astype(held_as)


def gaussian_with(own_key, dims, spread, reach, pieces, heavy, kind=jnp.bfloat16):
    array = spread * jax.random.normal(own_key, dims, jnp.float32)
    if pieces:
        array = array * level_of(own_key, dims, pieces, -0.22, 0.18)
    return jnp.clip(spiked(array, jax.random.fold_in(own_key, 3), *heavy), -reach, reach).astype(kind)


def setup_inputs(seed: int = 0) -> dict:
    key_of = jax.random.split(jax.random.key(seed), 6)
    return {
        "points": gaussian(key_of[0], (NPTS, D), 1.0, 6.0, ((0, 32),)),
        "factor": gaussian_with(key_of[1], (NPTS, K_HELD), (10 * K_HELD) ** -0.5, 0.078125, ((0, 32),), (0, 1, 32, 2.75)),
        "targets": gaussian(key_of[2], (NPTS, NT), 1.0, 6.0, ((0, 32),)),
        "pivot_slots": draw_pivot_slots(jax.random.fold_in(key_of[5], 71), 0),
        "pivot_counts": ragged(key_of[4], DEVICES, BLOCK, CAP, 2).astype(jnp.int32),
    }


sharpness = 1.0
ridge_shift = 0.01
damping = 1.0
epsilon = 1e-06

def normalize(points):
    values = points.astype(jnp.float32)
    factor_scale = lax.rsqrt(lax.optimization_barrier(jnp.mean(values * values, axis=1, keepdims=True)) + epsilon)
    return (values * factor_scale).astype(jnp.bfloat16)

def kernel(left_rows, right_rows, feature_width):
    cosine = lax.dot_general(left_rows.astype(jnp.float32), right_rows.astype(jnp.float32), (((1,), (1,)), ((), ())), preferred_element_type=jnp.float32) / feature_width
    return jnp.exp(sharpness * (cosine - 1.0))

def compact_index(pivot_counts, block_size):
    owners_count = pivot_counts.shape[0]
    run_ends = jnp.cumsum(pivot_counts).astype(jnp.int32)
    run_starts = (run_ends - pivot_counts).astype(jnp.int32)
    position = jnp.arange(block_size, dtype=jnp.int32)
    owners = lax.optimization_barrier(jnp.sum((position[:, None] >= run_ends[None, :]).astype(jnp.int32), axis=1)).astype(jnp.int32)
    onehot = (owners[:, None] == jnp.arange(owners_count, dtype=jnp.int32)[None, :]).astype(jnp.int32)
    first_row = lax.optimization_barrier(jnp.sum(onehot * run_starts[None, :], axis=1)).astype(jnp.int32)
    return (owners, (position - first_row).astype(jnp.int32))

def block_factor(pivot_scaled, pivot_factor):
    intersection = lax.dot_general(pivot_factor.astype(jnp.float32), pivot_factor.astype(jnp.float32), (((1,), (1,)), ((), ())), preferred_element_type=jnp.float32)
    diag_shift = ridge_shift + jnp.max(lax.optimization_barrier(jnp.sum(jnp.abs(intersection), axis=1)))
    ridged = kernel(pivot_scaled, pivot_scaled, pivot_scaled.shape[1]) - intersection + diag_shift * jnp.eye(intersection.shape[0], dtype=jnp.float32)
    return jnp.linalg.cholesky(ridged)

def reference(points, factor, targets, pivot_slots, pivot_counts):
    scaled = normalize(points)
    owners, slot_index = compact_index(pivot_counts, BLOCK)
    local_rows = pivot_slots[owners, slot_index].astype(jnp.int32)
    pivot_rows = (owners * PTS_DEV + local_rows).astype(jnp.int32)
    pivot_scaled = jnp.take(scaled, pivot_rows, axis=0)
    pivot_factor = jnp.take(factor, pivot_rows, axis=0)
    lower_factor = block_factor(pivot_scaled, pivot_factor)

    def columns(block_number):
        start_row = (block_number * PTS_DEV).astype(jnp.int32)
        part_scaled = lax.dynamic_slice_in_dim(scaled, start_row, PTS_DEV, 0)
        part_factor = lax.dynamic_slice_in_dim(factor, start_row, PTS_DEV, 0)
        downdated = kernel(pivot_scaled, part_scaled, part_scaled.shape[1]) - lax.dot_general(pivot_factor.astype(jnp.float32), part_factor.astype(jnp.float32), (((1,), (1,)), ((), ())), preferred_element_type=jnp.float32)
        return lax.linalg.triangular_solve(lower_factor, downdated, left_side=True, lower=True).astype(jnp.bfloat16)
    new_blocks = lax.map(columns, jnp.arange(NPTS // PTS_DEV, dtype=jnp.int32))
    new_columns = jnp.transpose(new_blocks, (1, 0, 2)).reshape(BLOCK, NPTS)
    cross_terms = jnp.concatenate([lax.dot_general(factor.astype(jnp.float32), targets.astype(jnp.float32), (((0,), (0,)), ((), ())), preferred_element_type=jnp.float32), lax.dot_general(new_columns.astype(jnp.float32), targets.astype(jnp.float32), (((1,), (0,)), ((), ())), preferred_element_type=jnp.float32)], axis=0)
    col_norms = jnp.concatenate([lax.optimization_barrier(jnp.sum(jnp.square(factor.astype(jnp.float32)), axis=0)), lax.optimization_barrier(jnp.sum(jnp.square(new_columns.astype(jnp.float32)), axis=1))], axis=0)
    coefficients = (cross_terms / (col_norms + damping)[:, None]).astype(jnp.bfloat16)
    fitted = jnp.dot(factor.astype(jnp.float32), coefficients[:K_HELD].astype(jnp.float32), preferred_element_type=jnp.float32)
    fitted = fitted + lax.dot_general(new_columns.astype(jnp.float32), coefficients[K_HELD:].astype(jnp.float32), (((0,), (0,)), ((), ())), preferred_element_type=jnp.float32)
    residual_next = targets.astype(jnp.float32) - fitted
    return (new_columns, residual_next)
```

```python
import functools

import jax
import jax.numpy as jnp
import numpy as np
from jax import lax
from jax.experimental import pallas as pl
from jax.experimental.pallas import tpu as pltpu
from jax.sharding import PartitionSpec as P

BLOCK = 512
TILE = 128

sharpness = 1.0
ridge_shift = 0.01
damping = 1.0
epsilon = 1e-06

f32 = jnp.float32
bf16 = jnp.bfloat16
AXES = ("row", "col")
VMEM = pl.BlockSpec(memory_space=pltpu.VMEM)
ANY = pl.BlockSpec(memory_space=pl.ANY)


def dot(a, b, da=1, db=0, exact=False):
    return lax.dot_general(
        a,
        b,
        (((da,), (db,)), ((), ())),
        precision=lax.Precision.HIGHEST if exact else None,
        preferred_element_type=f32,
    )


def split(v):
    high = v.astype(bf16)
    return high, (v - high.astype(f32)).astype(bf16)


def normalize(points):
    values = points.astype(f32)
    scale = lax.rsqrt(jnp.mean(values * values, axis=1, keepdims=True) + epsilon)
    return (values * scale).astype(bf16)


class Grid:
    def __init__(self, mesh):
        rows, cols = mesh.shape["row"], mesh.shape["col"]
        c = 2 if rows % 2 == 0 else 1
        x = max(k for k in range(1, cols + 1) if cols % k == 0 and k * k <= cols)
        self.n = {"y": rows // c, "c": c, "z": cols // x, "x": x}
        self.shape = tuple(self.n.values())
        self.size = rows * cols
        self.ids = np.arange(self.size).reshape(self.shape)

    def here(self):
        row, col = lax.axis_index("row"), lax.axis_index("col")
        c, x = self.n["c"], self.n["x"]
        return {"y": row // c, "c": row % c, "z": col // x, "x": col % x}

    def shift(self, value, dim, by):
        to = np.roll(self.ids, -by, axis=list(self.n).index(dim))
        return lax.ppermute(value, AXES, list(zip(self.ids.ravel(), to.ravel())))

    def spread(self, value, dim):
        return [self.shift(value, dim, s) for s in range(1, self.n[dim])]

    def reduce_scatter(self, chunks, dims):
        me, names = self.here(), list(self.n)
        for dim in dims:
            axis, n = names.index(dim), self.n[dim]

            def pick(k):
                return lax.dynamic_index_in_dim(chunks, k, names.index(dim), keepdims=True)

            total = pick(me[dim])
            for s in range(1, n):
                total = total + self.shift(pick((me[dim] + s) % n), dim, s)
            chunks = total
            del axis
        return chunks.reshape(chunks.shape[4:])

    def gather(self, chunk, dims):
        me, names = self.here(), list(self.n)
        whole = chunk[None, None, None, None]
        for dim in dims:
            axis, n = names.index(dim), self.n[dim]
            shape = list(whole.shape)
            shape[axis] = n
            out = jnp.zeros(shape, whole.dtype)
            for s in range(n):
                part = whole if s == 0 else self.shift(whole, dim, s)
                out = lax.dynamic_update_slice_in_dim(out, part, (me[dim] - s) % n, axis)
            whole = out
        return whole


ALIGN = 16


def own_rows_kernel(slots, points, factor, out, pbuf, fbuf, psem, fsem):
    cap = out.shape[0]
    width = points.shape[1]

    def copies(i):
        base = pl.multiple_of((slots[0, i] // ALIGN) * ALIGN, ALIGN)
        return (
            pltpu.make_async_copy(
                points.at[pl.ds(base, ALIGN), :], pbuf.at[pl.ds(i * ALIGN, ALIGN), :], psem.at[i]
            ),
            pltpu.make_async_copy(
                factor.at[pl.ds(base, ALIGN), :], fbuf.at[pl.ds(i * ALIGN, ALIGN), :], fsem.at[i]
            ),
        )

    for i in range(cap):
        for copy in copies(i):
            copy.start()
    r = lax.broadcasted_iota(jnp.int32, (cap, cap * ALIGN), 0)
    q = lax.broadcasted_iota(jnp.int32, (cap, cap * ALIGN), 1)
    target = jnp.full((cap, cap * ALIGN), -1, jnp.int32)
    for i in range(cap):
        target = jnp.where(r == i, slots[0, i] % ALIGN + i * ALIGN, target)
    pick = (q == target).astype(f32).astype(bf16)
    for i in range(cap):
        for copy in copies(i):
            copy.wait()
    rows = dot(pick, pbuf[...]).astype(bf16)
    out[:, :width] = normalize(rows)
    out[:, width:] = dot(pick, fbuf[...]).astype(bf16)


def own_rows(points, factor, slots):
    cap = slots.shape[1]
    wide = points.shape[1] + factor.shape[1]
    return pl.pallas_call(
        own_rows_kernel,
        out_shape=jax.ShapeDtypeStruct((cap, wide), bf16),
        in_specs=[pl.BlockSpec(memory_space=pltpu.SMEM), ANY, ANY],
        out_specs=VMEM,
        scratch_shapes=[
            pltpu.VMEM((cap * ALIGN, points.shape[1]), bf16),
            pltpu.VMEM((cap * ALIGN, factor.shape[1]), bf16),
            pltpu.SemaphoreType.DMA((cap,)),
            pltpu.SemaphoreType.DMA((cap,)),
        ],
        cost_estimate=pl.CostEstimate(flops=10**8, bytes_accessed=3 * 10**6, transcendentals=0),
    )(slots, points, factor)


def prepare_kernel(count, width, *refs):
    place, pieces = refs[0], refs[1 : 1 + count]
    scaled_ref, factor_ref, ridged_ref, rows, sems = refs[1 + count :]
    copies, at = [], 0
    for k, piece in enumerate(pieces):
        n = piece.shape[0]
        copies.append(pltpu.make_async_copy(piece, rows.at[pl.ds(at, n), :], sems.at[k]))
        at += n
    for copy in copies:
        copy.start()
    slot = lax.broadcasted_iota(jnp.int32, (BLOCK, at), 0)
    pick = (slot == place[...]).astype(f32).astype(bf16)
    for copy in copies:
        copy.wait()
    step = width
    for lo in range(0, rows.shape[1], step):
        part = dot(pick, rows[:, lo : lo + step]).astype(bf16)
        if lo == 0:
            scaled_ref[...] = part
        else:
            factor_ref[:, lo - width : lo - width + step] = part
    inter = dot(factor_ref[...], factor_ref[...], 1, 1)
    shift = ridge_shift + jnp.max(jnp.sum(jnp.abs(inter), axis=1, keepdims=True))
    cosine = dot(scaled_ref[...], scaled_ref[...], 1, 1) / width
    r = lax.broadcasted_iota(jnp.int32, (BLOCK, BLOCK), 0)
    c = lax.broadcasted_iota(jnp.int32, (BLOCK, BLOCK), 1)
    ridged_ref[...] = jnp.exp(sharpness * (cosine - 1.0)) - inter + jnp.where(r == c, shift, 0.0)


def prepare(place, pieces, width):
    wide = pieces[0].shape[1]
    total = sum(p.shape[0] for p in pieces)
    return pl.pallas_call(
        functools.partial(prepare_kernel, len(pieces), width),
        out_shape=(
            jax.ShapeDtypeStruct((BLOCK, width), bf16),
            jax.ShapeDtypeStruct((BLOCK, wide - width), bf16),
            jax.ShapeDtypeStruct((BLOCK, BLOCK), f32),
        ),
        in_specs=[VMEM] + [ANY] * len(pieces),
        out_specs=(VMEM,) * 3,
        scratch_shapes=[
            pltpu.VMEM((total, wide), bf16),
            pltpu.SemaphoreType.DMA((len(pieces),)),
        ],
        cost_estimate=pl.CostEstimate(
            flops=6 * 10**9, bytes_accessed=10**7, transcendentals=BLOCK * BLOCK
        ),
    )(place, *pieces)


def downdate_kernel(ps, pf, points, factor, targets, high_ref, low_ref, z_ref, acc):
    step = pl.program_id(0)
    cosine = dot(ps[...], normalize(points[...]), 1, 1) / ps.shape[1]
    down = jnp.exp(sharpness * (cosine - 1.0)) - dot(pf[...], factor[...], 1, 1)
    high, low = split(down)
    high_ref[...] = high
    low_ref[...] = low
    part = dot(high, targets[...]) + dot(low, targets[...])

    @pl.when(step == 0)
    def _():
        acc[...] = part

    @pl.when(step > 0)
    def _():
        acc[...] += part

    @pl.when(step == pl.num_programs(0) - 1)
    def _():
        z_ref[...] = acc[...].T


def downdate(ps, pf, points, factor, targets):
    pts, width, held, nt = points.shape[0], points.shape[1], factor.shape[1], targets.shape[1]
    blk = 256
    return pl.pallas_call(
        downdate_kernel,
        grid=(pts // blk,),
        out_shape=(
            jax.ShapeDtypeStruct((BLOCK, pts), bf16),
            jax.ShapeDtypeStruct((BLOCK, pts), bf16),
            jax.ShapeDtypeStruct((nt, BLOCK), f32),
        ),
        in_specs=[
            pl.BlockSpec((BLOCK, width), lambda i: (0, 0)),
            pl.BlockSpec((BLOCK, held), lambda i: (0, 0)),
            pl.BlockSpec((blk, width), lambda i: (i, 0)),
            pl.BlockSpec((blk, held), lambda i: (i, 0)),
            pl.BlockSpec((blk, nt), lambda i: (i, 0)),
        ],
        out_specs=(
            pl.BlockSpec((BLOCK, blk), lambda i: (0, i)),
            pl.BlockSpec((BLOCK, blk), lambda i: (0, i)),
            pl.BlockSpec((nt, BLOCK), lambda i: (0, 0)),
        ),
        scratch_shapes=[pltpu.VMEM((BLOCK, nt), f32)],
        cost_estimate=pl.CostEstimate(
            flops=6 * 10**9, bytes_accessed=16 * 10**6, transcendentals=BLOCK * pts
        ),
    )(ps, pf, points, factor, targets)


def across(v):
    return jnp.broadcast_to(v, (8, TILE))


def base8(tile, lane0):
    e = [[None] * 8 for _ in range(8)]
    for s in range(8):
        col = across(tile[:, lane0 + s : lane0 + s + 1])
        for t in range(s, 8):
            e[t][s] = across(col[t : t + 1, :])
    x = [[None] * 8 for _ in range(8)]
    low = [[None] * 8 for _ in range(8)]
    for s in range(8):
        r = lax.rsqrt(e[s][s])
        for t in range(s + 1, 8):
            low[t][s] = e[t][s] * r
        for u in range(s + 1, 8):
            for t in range(u, 8):
                e[t][u] = e[t][u] - low[t][s] * low[u][s]
        for c in range(s):
            acc = low[s][c] * x[c][c]
            for u in range(c + 1, s):
                acc = acc + low[s][u] * x[u][c]
            x[s][c] = -(r * acc)
        x[s][s] = r
    return x


def columns(x, rowid):
    out = []
    for s in range(8):
        c = jnp.where(rowid == s, x[s][s], 0.0)
        for t in range(s + 1, 8):
            c = jnp.where(rowid == t, x[t][s], c)
        out.append(c)
    return out


def diagonal_block(s_ref, w_ref):
    n, group = TILE, 32
    rowid = lax.broadcasted_iota(jnp.int32, (8, n), 0)
    ri = lax.broadcasted_iota(jnp.int32, (n, n), 0)
    ci = lax.broadcasted_iota(jnp.int32, (n, n), 1)
    w_ref[...] = jnp.where(ri == ci, 1.0, 0.0).astype(f32)
    for g in range(0, n, group):
        tiles = [s_ref[g + 8 * i : g + 8 * i + 8, :] for i in range(4)]
        sides = [w_ref[g + 8 * i : g + 8 * i + 8, :] for i in range(4)]
        for j in range(4):
            lane0 = g + 8 * j
            x = base8(tiles[j], lane0)
            cols = columns(x, rowid)
            u = cols[0] * across(tiles[j][0:1, :])
            q = cols[0] * across(sides[j][0:1, :])
            for s in range(1, 8):
                u = u + cols[s] * across(tiles[j][s : s + 1, :])
                q = q + cols[s] * across(sides[j][s : s + 1, :])
            tiles[j], sides[j] = u, q
            for i in range(j + 1, 4):
                b = [across(tiles[i][:, lane0 + k : lane0 + k + 1]) for k in range(8)]
                t, v = tiles[i], sides[i]
                for s in range(8):
                    m = x[s][0] * b[0]
                    for k in range(1, s + 1):
                        m = m + x[s][k] * b[k]
                    t = t - m * across(u[s : s + 1, :])
                    v = v - m * across(q[s : s + 1, :])
                tiles[i], sides[i] = t, v
        ug = jnp.concatenate(tiles, 0)
        vg = jnp.concatenate(sides, 0)
        w_ref[g : g + group, :] = vg
        if g + group < n:
            lo = g + group
            upd = dot(ug, jnp.concatenate([ug, vg], 1), 0, 0, exact=True)
            s_ref[lo:, :] = s_ref[lo:, :] - upd[lo:, :n]
            w_ref[lo:, :] = w_ref[lo:, :] - upd[lo:, n:]


def factor_kernel(first, last, a_in, r_in, a_ref, r_ref, s_ref, w_ref):
    n, blocks = TILE, BLOCK // TILE
    a_ref[...] = a_in[...]
    r_ref[...] = r_in[...]
    for k in range(first, last):
        o = n * k
        s_ref[...] = a_ref[o : o + n, o : o + n]
        diagonal_block(s_ref, w_ref)
        inv = w_ref[...]
        if k:
            r_ref[o : o + n, :o] = dot(inv, r_ref[o : o + n, :o], exact=True)
        r_ref[o : o + n, o : o + n] = inv
        if k < blocks - 1:
            u = dot(inv, a_ref[o : o + n, o + n :], exact=True)
            wk = r_ref[o : o + n, : o + n]
            a_ref[o + n :, o + n :] = a_ref[o + n :, o + n :] - dot(u, u, 0, 0, exact=True)
            r_ref[o + n :, : o + n] = r_ref[o + n :, : o + n] - dot(u, wk, 0, 0, exact=True)


def factor_step(a, r, first, last):
    return pl.pallas_call(
        functools.partial(factor_kernel, first, last),
        out_shape=(jax.ShapeDtypeStruct(a.shape, f32),) * 2,
        in_specs=[VMEM] * 2,
        out_specs=(VMEM,) * 2,
        scratch_shapes=[pltpu.VMEM((TILE, TILE), f32)] * 2,
        input_output_aliases={0: 0, 1: 1},
        cost_estimate=pl.CostEstimate(
            flops=12 * 10**9, bytes_accessed=4 * 10**6, transcendentals=0
        ),
    )(a, r)


def columns_kernel(inv, z, high, low, new_ref, cross_ref, norm_ref, acc, ih, il):
    step = pl.program_id(0)

    @pl.when(step == 0)
    def _():
        ih[...], il[...] = split(inv[...])
        cross_ref[...] = dot(z[...], inv[...], 1, 1, exact=True)

    h = high[...]
    new = (dot(ih[...], h) + (dot(ih[...], low[...]) + dot(il[...], h))).astype(bf16)
    new_ref[...] = new
    wide = new.astype(f32)
    part = wide * wide

    @pl.when(step == 0)
    def _():
        acc[...] = part

    @pl.when(step > 0)
    def _():
        acc[...] += part

    @pl.when(step == pl.num_programs(0) - 1)
    def _():
        norm_ref[...] = jnp.sum(acc[...].T, axis=0, keepdims=True)


def make_columns(inv, z, high, low):
    pts, blk = high.shape[1], 256
    return pl.pallas_call(
        columns_kernel,
        grid=(pts // blk,),
        out_shape=(
            jax.ShapeDtypeStruct((BLOCK, pts), bf16),
            jax.ShapeDtypeStruct(z.shape, f32),
            jax.ShapeDtypeStruct((1, BLOCK), f32),
        ),
        in_specs=[
            pl.BlockSpec((BLOCK, BLOCK), lambda i: (0, 0)),
            pl.BlockSpec(z.shape, lambda i: (0, 0)),
            pl.BlockSpec((BLOCK, blk), lambda i: (0, i)),
            pl.BlockSpec((BLOCK, blk), lambda i: (0, i)),
        ],
        out_specs=(
            pl.BlockSpec((BLOCK, blk), lambda i: (0, i)),
            pl.BlockSpec(z.shape, lambda i: (0, 0)),
            pl.BlockSpec((1, BLOCK), lambda i: (0, 0)),
        ),
        scratch_shapes=[
            pltpu.VMEM((BLOCK, blk), f32),
            pltpu.VMEM((BLOCK, BLOCK), bf16),
            pltpu.VMEM((BLOCK, BLOCK), bf16),
        ],
        cost_estimate=pl.CostEstimate(
            flops=4 * 10**9, bytes_accessed=8 * 10**6, transcendentals=0
        ),
    )(inv, z, high, low)


def on_device(grid, points, factor, targets, pivot_slots, pivot_counts):
    n, me = grid.n, grid.here()
    cap, devices = pivot_slots.shape[1], grid.size
    held, nt, width = factor.shape[1], targets.shape[1], points.shape[1]

    own = own_rows(points, factor, pivot_slots)
    blocks = [own] + grid.spread(own, "z")
    zs = [(0, 0, s, 0) for s in range(n["z"])]
    half = (n["z"] + 1) // 2

    def moved(origin, dim):
        at = "yczx".index(dim)
        return [
            tuple(v + s if k == at else v for k, v in enumerate(o))
            for s in range(1, n[dim])
            for o in origin
        ]

    pieces, origins = [jnp.concatenate(blocks, 0)], list(zs)
    for part, origin, dims in (
        (blocks[:half], zs[:half], "xy"),
        (blocks[half:], zs[half:], "yx"),
    ):
        if not part:
            continue
        held_here, held_origin = jnp.concatenate(part, 0), origin
        for dim in dims:
            if n[dim] == 1:
                continue
            got = grid.spread(held_here, dim)
            arrived = jnp.concatenate(got, 0) if len(got) > 1 else got[0]
            new_origin = moved(held_origin, dim)
            pieces.append(arrived)
            origins += new_origin
            held_here = jnp.concatenate([held_here, arrived], 0)
            held_origin = held_origin + new_origin
    zdone = pieces[0]
    mine = list(pieces)
    for s in range(1, n["c"]):
        pieces += [grid.shift(p, "c", s) for p in mine]
        origins += [(o[0], o[1] + s, o[2], o[3]) for o in origins[: len(origins)]]

    shifts = np.array(origins)
    dev = jnp.zeros((len(origins),), jnp.int32)
    for k, dim in enumerate("yczx"):
        dev = dev * n[dim] + (me[dim] - shifts[:, k]) % n[dim]
    ends = jnp.cumsum(pivot_counts)
    onehot = dev[:, None] == jnp.arange(devices, dtype=jnp.int32)[None, :]
    count = jnp.sum(jnp.where(onehot, pivot_counts[None, :], 0), axis=1)
    start = jnp.sum(jnp.where(onehot, (ends - pivot_counts)[None, :], 0), axis=1)
    slot = jnp.arange(cap, dtype=jnp.int32)[None, :]
    place = jnp.where(slot < count[:, None], start[:, None] + slot, -1).reshape(1, -1)

    cross = dot(factor, targets, 0, 0)
    squares = jnp.sum(jnp.square(factor.astype(f32)), axis=0)
    m = held // devices
    extra = 8 * -(-m // (8 * nt))
    chunks = jnp.concatenate(
        [
            cross.reshape(devices, m, nt),
            jnp.pad(squares.reshape(devices, m), ((0, 0), (0, extra * nt - m))).reshape(
                devices, extra, nt
            ),
        ],
        axis=1,
    )
    chunks, zdone = lax.optimization_barrier((chunks, zdone))
    chunk = grid.reduce_scatter(chunks.reshape(grid.shape + chunks.shape[1:]), "czxy")
    norm = chunk[m:].reshape(-1)[:m]
    coef = (chunk[:m] / (norm + damping)[:, None]).astype(bf16)
    coef_held = grid.gather(coef, "zxyc").reshape(held, nt)

    ps, pf, ridged = prepare(place, pieces, width)
    high, low, z = downdate(ps, pf, points, factor, targets)
    t = nt // devices
    z_own = grid.reduce_scatter(z.reshape(grid.shape + (t, BLOCK)), "cxyz")

    inverse = jnp.zeros((BLOCK, BLOCK), f32)
    middle = BLOCK // TILE // 2
    ridged, inverse = factor_step(ridged, inverse, 0, middle)
    ridged, inverse = factor_step(ridged, inverse, middle, BLOCK // TILE)

    new_columns, cross_own, norm_own = make_columns(inverse, z_own, high, low)
    nh, nl = split(norm_own)
    nl2 = (norm_own - nh.astype(f32) - nl.astype(f32)).astype(bf16)
    late = jnp.concatenate([cross_own.astype(bf16), nh, nl, nl2], axis=0)
    late = jnp.pad(late, ((0, -late.shape[0] % 16), (0, 0)))
    every = lax.all_to_all(
        jnp.broadcast_to(late[None], (devices,) + late.shape), AXES, 0, 0, tiled=True
    ).astype(f32)
    norm_new = jnp.sum(every[:, t : t + 3], axis=(0, 1))
    coef_new = (every[:, :t].reshape(nt, BLOCK) / (norm_new + damping)[None, :]).astype(bf16)

    fitted = jnp.dot(factor, coef_held, preferred_element_type=f32)
    fitted = fitted + dot(new_columns, coef_new, 0, 1)
    return new_columns, targets.astype(f32) - fitted


def solution(mesh):
    spec = P(AXES, None)
    return jax.shard_map(
        functools.partial(on_device, Grid(mesh)),
        mesh=mesh,
        in_specs=(spec, spec, spec, spec, P()),
        out_specs=(P(None, AXES), spec),
        check_vma=False,
    )
```

```python
import functools

import jax
import jax.numpy as jnp
import numpy as np
from jax import lax
from jax.experimental import pallas as pl
from jax.experimental.pallas import tpu as pltpu
from jax.sharding import PartitionSpec as P

BLOCK = 512
TILE = 128


sharpness = 1.0
ridge_shift = 0.01
damping = 1.0
epsilon = 1e-06

f32 = jnp.float32
bf16 = jnp.bfloat16
AXES = ("row", "col")
VMEM = pl.BlockSpec(memory_space=pltpu.VMEM)
ANY = pl.BlockSpec(memory_space=pl.ANY)


def dot(a, b, da=1, db=0, exact=False):
    return lax.dot_general(
        a,
        b,
        (((da,), (db,)), ((), ())),
        precision=lax.Precision.HIGHEST if exact else None,
        preferred_element_type=f32,
    )


def split(v):
    high = v.astype(bf16)
    return high, (v - high.astype(f32)).astype(bf16)


def normalize(points):
    values = points.astype(f32)
    scale = lax.rsqrt(jnp.mean(values * values, axis=1, keepdims=True) + epsilon)
    return (values * scale).astype(bf16)


class Grid:
    def __init__(self, mesh):
        rows, cols = mesh.shape["row"], mesh.shape["col"]
        c = 2 if rows % 2 == 0 else 1
        x = max(k for k in range(1, cols + 1) if cols % k == 0 and k * k <= cols)
        self.n = {"y": rows // c, "c": c, "z": cols // x, "x": x}
        self.shape = tuple(self.n.values())
        self.size = rows * cols
        self.ids = np.arange(self.size).reshape(self.shape)

    def here(self):
        row, col = lax.axis_index("row"), lax.axis_index("col")
        c, x = self.n["c"], self.n["x"]
        return {"y": row // c, "c": row % c, "z": col // x, "x": col % x}

    def shift(self, value, dim, by):
        to = np.roll(self.ids, -by, axis=list(self.n).index(dim))
        return lax.ppermute(value, AXES, list(zip(self.ids.ravel(), to.ravel())))

    def spread(self, value, dim):
        return [self.shift(value, dim, s) for s in range(1, self.n[dim])]

    def take(self, chunks, dim, by=0):
        at = (self.here()[dim] + by) % self.n[dim]
        return lax.dynamic_index_in_dim(chunks, at, list(self.n).index(dim), keepdims=True)

    def sends(self, chunks, dim):
        return [self.take(chunks, dim, s) for s in range(1, self.n[dim])]

    def reduce(self, chunks, dim, sends=None):
        total = self.take(chunks, dim)
        for s, part in enumerate(sends or self.sends(chunks, dim), 1):
            total = total + self.shift(part, dim, s).astype(f32)
        return total

    def exchange(self, parts):
        return lax.all_to_all(parts, AXES, 0, 0, tiled=True)

    def everywhere(self, part):
        return self.exchange(jnp.broadcast_to(part[None], (self.size,) + part.shape))


ALIGN = 16


def own_rows_kernel(slots, points, factor, out, pbuf, fbuf, psem, fsem):
    cap = out.shape[0]
    width = points.shape[1]

    def copies(i):
        base = pl.multiple_of((slots[0, i] // ALIGN) * ALIGN, ALIGN)
        return (
            pltpu.make_async_copy(
                points.at[pl.ds(base, ALIGN), :], pbuf.at[pl.ds(i * ALIGN, ALIGN), :], psem.at[i]
            ),
            pltpu.make_async_copy(
                factor.at[pl.ds(base, ALIGN), :], fbuf.at[pl.ds(i * ALIGN, ALIGN), :], fsem.at[i]
            ),
        )

    for i in range(cap):
        for copy in copies(i):
            copy.start()
    r = lax.broadcasted_iota(jnp.int32, (cap, cap * ALIGN), 0)
    q = lax.broadcasted_iota(jnp.int32, (cap, cap * ALIGN), 1)
    target = jnp.full((cap, cap * ALIGN), -1, jnp.int32)
    for i in range(cap):
        target = jnp.where(r == i, slots[0, i] % ALIGN + i * ALIGN, target)
    pick = (q == target).astype(f32).astype(bf16)
    for i in range(cap):
        for copy in copies(i):
            copy.wait()
    rows = dot(pick, pbuf[...]).astype(bf16)
    out[:, :width] = normalize(rows)
    out[:, width:] = dot(pick, fbuf[...]).astype(bf16)


def own_rows(points, factor, slots):
    cap = slots.shape[1]
    wide = points.shape[1] + factor.shape[1]
    return pl.pallas_call(
        own_rows_kernel,
        out_shape=jax.ShapeDtypeStruct((cap, wide), bf16),
        in_specs=[pl.BlockSpec(memory_space=pltpu.SMEM), ANY, ANY],
        out_specs=VMEM,
        scratch_shapes=[
            pltpu.VMEM((cap * ALIGN, points.shape[1]), bf16),
            pltpu.VMEM((cap * ALIGN, factor.shape[1]), bf16),
            pltpu.SemaphoreType.DMA((cap,)),
            pltpu.SemaphoreType.DMA((cap,)),
        ],
        cost_estimate=pl.CostEstimate(flops=10**8, bytes_accessed=3 * 10**6, transcendentals=0),
    )(slots, points, factor)


def prepare_kernel(count, width, *refs):
    place, pieces = refs[0], refs[1 : 1 + count]
    scaled_ref, factor_ref, ridged_ref, rows, sems = refs[1 + count :]
    copies, at = [], 0
    for k, piece in enumerate(pieces):
        n = piece.shape[0]
        copies.append(pltpu.make_async_copy(piece, rows.at[pl.ds(at, n), :], sems.at[k]))
        at += n
    for copy in copies:
        copy.start()
    slot = lax.broadcasted_iota(jnp.int32, (BLOCK, at), 0)
    pick = (slot == place[...]).astype(f32).astype(bf16)
    for copy in copies:
        copy.wait()
    step = width
    for lo in range(0, rows.shape[1], step):
        part = dot(pick, rows[:, lo : lo + step]).astype(bf16)
        if lo == 0:
            scaled_ref[...] = part
        else:
            factor_ref[:, lo - width : lo - width + step] = part
    inter = dot(factor_ref[...], factor_ref[...], 1, 1)
    shift = ridge_shift + jnp.max(jnp.sum(jnp.abs(inter), axis=1, keepdims=True))
    cosine = dot(scaled_ref[...], scaled_ref[...], 1, 1) / width
    r = lax.broadcasted_iota(jnp.int32, (BLOCK, BLOCK), 0)
    c = lax.broadcasted_iota(jnp.int32, (BLOCK, BLOCK), 1)
    ridged_ref[...] = jnp.exp(sharpness * (cosine - 1.0)) - inter + jnp.where(r == c, shift, 0.0)


def prepare(place, pieces, width):
    wide = pieces[0].shape[1]
    total = sum(p.shape[0] for p in pieces)
    return pl.pallas_call(
        functools.partial(prepare_kernel, len(pieces), width),
        out_shape=(
            jax.ShapeDtypeStruct((BLOCK, width), bf16),
            jax.ShapeDtypeStruct((BLOCK, wide - width), bf16),
            jax.ShapeDtypeStruct((BLOCK, BLOCK), f32),
        ),
        in_specs=[VMEM] + [ANY] * len(pieces),
        out_specs=(VMEM,) * 3,
        scratch_shapes=[
            pltpu.VMEM((total, wide), bf16),
            pltpu.SemaphoreType.DMA((len(pieces),)),
        ],
        cost_estimate=pl.CostEstimate(
            flops=6 * 10**9, bytes_accessed=10**7, transcendentals=BLOCK * BLOCK
        ),
    )(place, *pieces)


def downdate_kernel(ps, pf, points, factor, targets, high_ref, low_ref, z_ref, acc):
    step = pl.program_id(0)
    cosine = dot(ps[...], normalize(points[...]), 1, 1) / ps.shape[1]
    down = jnp.exp(sharpness * (cosine - 1.0)) - dot(pf[...], factor[...], 1, 1)
    high, low = split(down)
    high_ref[...] = high
    low_ref[...] = low
    part = dot(high, targets[...]) + dot(low, targets[...])

    @pl.when(step == 0)
    def _():
        acc[...] = part

    @pl.when(step > 0)
    def _():
        acc[...] += part

    @pl.when(step == pl.num_programs(0) - 1)
    def _():
        z_ref[...] = acc[...].T


def downdate(ps, pf, points, factor, targets):
    pts, width, held, nt = points.shape[0], points.shape[1], factor.shape[1], targets.shape[1]
    blk = 256
    return pl.pallas_call(
        downdate_kernel,
        grid=(pts // blk,),
        out_shape=(
            jax.ShapeDtypeStruct((BLOCK, pts), bf16),
            jax.ShapeDtypeStruct((BLOCK, pts), bf16),
            jax.ShapeDtypeStruct((nt, BLOCK), f32),
        ),
        in_specs=[
            pl.BlockSpec((BLOCK, width), lambda i: (0, 0)),
            pl.BlockSpec((BLOCK, held), lambda i: (0, 0)),
            pl.BlockSpec((blk, width), lambda i: (i, 0)),
            pl.BlockSpec((blk, held), lambda i: (i, 0)),
            pl.BlockSpec((blk, nt), lambda i: (i, 0)),
        ],
        out_specs=(
            pl.BlockSpec((BLOCK, blk), lambda i: (0, i)),
            pl.BlockSpec((BLOCK, blk), lambda i: (0, i)),
            pl.BlockSpec((nt, BLOCK), lambda i: (0, 0)),
        ),
        scratch_shapes=[pltpu.VMEM((BLOCK, nt), f32)],
        cost_estimate=pl.CostEstimate(
            flops=6 * 10**9, bytes_accessed=16 * 10**6, transcendentals=BLOCK * pts
        ),
    )(ps, pf, points, factor, targets)


def across(v):
    return jnp.broadcast_to(v, (8, TILE))


def base8(tile, lane0):
    e = [[None] * 8 for _ in range(8)]
    for s in range(8):
        col = across(tile[:, lane0 + s : lane0 + s + 1])
        for t in range(s, 8):
            e[t][s] = across(col[t : t + 1, :])
    x = [[None] * 8 for _ in range(8)]
    low = [[None] * 8 for _ in range(8)]
    for s in range(8):
        r = lax.rsqrt(e[s][s])
        for t in range(s + 1, 8):
            low[t][s] = e[t][s] * r
        for u in range(s + 1, 8):
            for t in range(u, 8):
                e[t][u] = e[t][u] - low[t][s] * low[u][s]
        for c in range(s):
            acc = low[s][c] * x[c][c]
            for u in range(c + 1, s):
                acc = acc + low[s][u] * x[u][c]
            x[s][c] = -(r * acc)
        x[s][s] = r
    return x


def columns(x, rowid):
    out = []
    for s in range(8):
        c = jnp.where(rowid == s, x[s][s], 0.0)
        for t in range(s + 1, 8):
            c = jnp.where(rowid == t, x[t][s], c)
        out.append(c)
    return out


def diagonal_block(s_ref, w_ref):
    n, group = TILE, 32
    rowid = lax.broadcasted_iota(jnp.int32, (8, n), 0)
    ri = lax.broadcasted_iota(jnp.int32, (n, n), 0)
    ci = lax.broadcasted_iota(jnp.int32, (n, n), 1)
    w_ref[...] = jnp.where(ri == ci, 1.0, 0.0).astype(f32)
    for g in range(0, n, group):
        tiles = [s_ref[g + 8 * i : g + 8 * i + 8, :] for i in range(4)]
        sides = [w_ref[g + 8 * i : g + 8 * i + 8, :] for i in range(4)]
        for j in range(4):
            lane0 = g + 8 * j
            x = base8(tiles[j], lane0)
            cols = columns(x, rowid)
            u = cols[0] * across(tiles[j][0:1, :])
            q = cols[0] * across(sides[j][0:1, :])
            for s in range(1, 8):
                u = u + cols[s] * across(tiles[j][s : s + 1, :])
                q = q + cols[s] * across(sides[j][s : s + 1, :])
            tiles[j], sides[j] = u, q
            for i in range(j + 1, 4):
                b = [across(tiles[i][:, lane0 + k : lane0 + k + 1]) for k in range(8)]
                t, v = tiles[i], sides[i]
                for s in range(8):
                    m = x[s][0] * b[0]
                    for k in range(1, s + 1):
                        m = m + x[s][k] * b[k]
                    t = t - m * across(u[s : s + 1, :])
                    v = v - m * across(q[s : s + 1, :])
                tiles[i], sides[i] = t, v
        ug = jnp.concatenate(tiles, 0)
        vg = jnp.concatenate(sides, 0)
        w_ref[g : g + group, :] = vg
        if g + group < n:
            lo = g + group
            upd = dot(ug, jnp.concatenate([ug, vg], 1), 0, 0, exact=True)
            s_ref[lo:, :] = s_ref[lo:, :] - upd[lo:, :n]
            w_ref[lo:, :] = w_ref[lo:, :] - upd[lo:, n:]


def factor_kernel(first, last, a_in, r_in, a_ref, r_ref, s_ref, w_ref):
    n, blocks = TILE, BLOCK // TILE
    a_ref[...] = a_in[...]
    r_ref[...] = r_in[...]
    for k in range(first, last):
        o = n * k
        s_ref[...] = a_ref[o : o + n, o : o + n]
        diagonal_block(s_ref, w_ref)
        inv = w_ref[...]
        if k:
            r_ref[o : o + n, :o] = dot(inv, r_ref[o : o + n, :o], exact=True)
        r_ref[o : o + n, o : o + n] = inv
        if k < blocks - 1:
            u = dot(inv, a_ref[o : o + n, o + n :], exact=True)
            wk = r_ref[o : o + n, : o + n]
            a_ref[o + n :, o + n :] = a_ref[o + n :, o + n :] - dot(u, u, 0, 0, exact=True)
            r_ref[o + n :, : o + n] = r_ref[o + n :, : o + n] - dot(u, wk, 0, 0, exact=True)


def factor_step(a, r, first, last):
    return pl.pallas_call(
        functools.partial(factor_kernel, first, last),
        out_shape=(jax.ShapeDtypeStruct(a.shape, f32),) * 2,
        in_specs=[VMEM] * 2,
        out_specs=(VMEM,) * 2,
        scratch_shapes=[pltpu.VMEM((TILE, TILE), f32)] * 2,
        input_output_aliases={0: 0, 1: 1},
        cost_estimate=pl.CostEstimate(
            flops=12 * 10**9, bytes_accessed=4 * 10**6, transcendentals=0
        ),
    )(a, r)


def columns_kernel(inv, z, high, low, new_ref, cross_ref, norm_ref, acc, ih, il):
    step = pl.program_id(0)

    @pl.when(step == 0)
    def _():
        ih[...], il[...] = split(inv[...])
        cross_ref[...] = dot(z[...], inv[...], 1, 1, exact=True)

    h = high[...]
    new = (dot(ih[...], h) + (dot(ih[...], low[...]) + dot(il[...], h))).astype(bf16)
    new_ref[...] = new
    wide = new.astype(f32)
    part = wide * wide

    @pl.when(step == 0)
    def _():
        acc[...] = part

    @pl.when(step > 0)
    def _():
        acc[...] += part

    @pl.when(step == pl.num_programs(0) - 1)
    def _():
        norm_ref[...] = jnp.sum(acc[...].T, axis=0, keepdims=True)


def make_columns(inv, z, high, low):
    pts, blk = high.shape[1], 256
    return pl.pallas_call(
        columns_kernel,
        grid=(pts // blk,),
        out_shape=(
            jax.ShapeDtypeStruct((BLOCK, pts), bf16),
            jax.ShapeDtypeStruct(z.shape, f32),
            jax.ShapeDtypeStruct((1, BLOCK), f32),
        ),
        in_specs=[
            pl.BlockSpec((BLOCK, BLOCK), lambda i: (0, 0)),
            pl.BlockSpec(z.shape, lambda i: (0, 0)),
            pl.BlockSpec((BLOCK, blk), lambda i: (0, i)),
            pl.BlockSpec((BLOCK, blk), lambda i: (0, i)),
        ],
        out_specs=(
            pl.BlockSpec((BLOCK, blk), lambda i: (0, i)),
            pl.BlockSpec(z.shape, lambda i: (0, 0)),
            pl.BlockSpec((1, BLOCK), lambda i: (0, 0)),
        ),
        scratch_shapes=[
            pltpu.VMEM((BLOCK, blk), f32),
            pltpu.VMEM((BLOCK, BLOCK), bf16),
            pltpu.VMEM((BLOCK, BLOCK), bf16),
        ],
        cost_estimate=pl.CostEstimate(
            flops=4 * 10**9, bytes_accessed=8 * 10**6, transcendentals=0
        ),
    )(inv, z, high, low)


def on_device(grid, points, factor, targets, pivot_slots, pivot_counts):
    n, me = grid.n, grid.here()
    cap, devices = pivot_slots.shape[1], grid.size
    held, nt, width = factor.shape[1], targets.shape[1], points.shape[1]

    own = own_rows(points, factor, pivot_slots)
    own, late_factor = lax.optimization_barrier((own, factor))
    cross = dot(late_factor, targets, 0, 0)
    squares = jnp.sum(jnp.square(late_factor.astype(f32)), axis=0)
    m = held // devices
    extra = 8 * -(-m // (8 * nt))
    chunks = jnp.concatenate(
        [
            cross.reshape(devices, m, nt),
            jnp.pad(squares.reshape(devices, m), ((0, 0), (0, extra * nt - m))).reshape(
                devices, extra, nt
            ),
        ],
        axis=1,
    )
    chunks = grid.reduce(chunks.reshape(grid.shape + chunks.shape[1:]), "c")
    sends = [part.astype(bf16) for part in grid.sends(chunks, "z")]

    arrived = grid.spread(own, "z")
    along_z = jnp.concatenate([own] + arrived, 0)
    along_z, sends = lax.optimization_barrier((along_z, sends))
    zs = [(0, 0, s, 0) for s in range(n["z"])]

    def moved(origin, dim, s):
        at = "yczx".index(dim)
        return [tuple(v + s if k == at else v for k, v in enumerate(o)) for o in origin]

    pieces, origins = [along_z], list(zs)
    by_x, by_y = grid.spread(along_z, "x"), grid.spread(along_z, "y")
    pieces += by_x + by_y
    for s in range(1, n["x"]):
        origins += moved(zs, "x", s)
    for s in range(1, n["y"]):
        origins += moved(zs, "y", s)
    chunks = grid.reduce(chunks, "z", sends)
    half = (n["z"] + 1) // 2
    for s, block in enumerate(by_x, 1):
        pieces += grid.spread(block[: half * cap], "y")
        for r in range(1, n["y"]):
            origins += moved(moved(zs[:half], "x", s), "y", r)
    for r, block in enumerate(by_y, 1):
        if half < n["z"]:
            pieces += grid.spread(block[half * cap :], "x")
            for s in range(1, n["x"]):
                origins += moved(moved(zs[half:], "x", s), "y", r)
    mine, mine_origins = list(pieces), list(origins)
    for s in range(1, n["c"]):
        pieces += [grid.shift(p, "c", s) for p in mine]
        origins += moved(mine_origins, "c", s)

    shifts = np.array(origins)
    dev = jnp.zeros((len(origins),), jnp.int32)
    for k, dim in enumerate("yczx"):
        dev = dev * n[dim] + (me[dim] - shifts[:, k]) % n[dim]
    ends = jnp.cumsum(pivot_counts)
    onehot = dev[:, None] == jnp.arange(devices, dtype=jnp.int32)[None, :]
    count = jnp.sum(jnp.where(onehot, pivot_counts[None, :], 0), axis=1)
    start = jnp.sum(jnp.where(onehot, (ends - pivot_counts)[None, :], 0), axis=1)
    slot = jnp.arange(cap, dtype=jnp.int32)[None, :]
    place = jnp.where(slot < count[:, None], start[:, None] + slot, -1).reshape(1, -1)

    for dim in "xy":
        sends = [part.astype(bf16) for part in grid.sends(chunks, dim)]
        chunks = grid.reduce(chunks, dim, sends)
    chunks = chunks.reshape(m + extra, nt)
    norm = chunks[m:].reshape(-1)[:m]
    coef = (chunks[:m] / (norm + damping)[:, None]).astype(bf16)
    coef = jnp.broadcast_to(coef[None], (devices,) + coef.shape)

    place, coef = lax.optimization_barrier((place, coef))
    ps, pf, ridged = prepare(place, pieces, width)
    high, low, z = downdate(ps, pf, points, factor, targets)
    t = nt // devices
    coef_held = grid.exchange(coef)
    z, coef_held = lax.optimization_barrier((z, coef_held))
    coef_held = coef_held.reshape(held, nt)
    z_parts = grid.exchange(z.reshape(devices, t, BLOCK))
    z_own = jnp.sum(z_parts, axis=0)

    inverse = jnp.zeros((BLOCK, BLOCK), f32)
    middle = BLOCK // TILE // 2
    ridged, inverse = factor_step(ridged, inverse, 0, middle)
    ridged, inverse = factor_step(ridged, inverse, middle, BLOCK // TILE)

    new_columns, cross_own, norm_own = make_columns(inverse, z_own, high, low)
    nh, nl = split(norm_own)
    nl2 = (norm_own - nh.astype(f32) - nl.astype(f32)).astype(bf16)
    late = jnp.concatenate([cross_own.astype(bf16), nh, nl, nl2], axis=0)
    late = jnp.pad(late, ((0, -late.shape[0] % 16), (0, 0)))
    every = grid.everywhere(late).astype(f32)
    norm_new = jnp.sum(every[:, t : t + 3], axis=(0, 1))
    coef_new = (every[:, :t].reshape(nt, BLOCK) / (norm_new + damping)[None, :]).astype(bf16)

    fitted = dot(factor, coef_held)
    fitted = fitted + dot(new_columns, coef_new, 0, 1)
    return new_columns, targets.astype(f32) - fitted


def step(grid, *args):
    return on_device(grid, *args)


def solution(mesh):
    spec = P(AXES, None)
    return jax.shard_map(
        functools.partial(step, Grid(mesh)),
        mesh=mesh,
        in_specs=(spec, spec, spec, spec, P()),
        out_specs=(P(None, AXES), spec),
        check_vma=False,
    )
```

```python
import functools

import jax
import jax.numpy as jnp
import numpy as np
from jax import lax
from jax.experimental import pallas as pl
from jax.experimental.pallas import tpu as pltpu
from jax.sharding import PartitionSpec as P

BLOCK = 512
TILE = 128


sharpness = 1.0
ridge_shift = 0.01
damping = 1.0
epsilon = 1e-06

f32 = jnp.float32
bf16 = jnp.bfloat16
AXES = ("row", "col")
VMEM = pl.BlockSpec(memory_space=pltpu.VMEM)
ANY = pl.BlockSpec(memory_space=pl.ANY)


def dot(a, b, da=1, db=0, exact=False):
    return lax.dot_general(
        a,
        b,
        (((da,), (db,)), ((), ())),
        precision=lax.Precision.HIGHEST if exact else None,
        preferred_element_type=f32,
    )


def split(v):
    high = v.astype(bf16)
    return high, (v - high.astype(f32)).astype(bf16)


def normalize(points):
    values = points.astype(f32)
    scale = lax.rsqrt(jnp.mean(values * values, axis=1, keepdims=True) + epsilon)
    return (values * scale).astype(bf16)


class Grid:
    def __init__(self, mesh):
        rows, cols = mesh.shape["row"], mesh.shape["col"]
        c = 2 if rows % 2 == 0 else 1
        x = max(k for k in range(1, cols + 1) if cols % k == 0 and k * k <= cols)
        self.n = {"y": rows // c, "c": c, "z": cols // x, "x": x}
        self.shape = tuple(self.n.values())
        self.size = rows * cols
        self.ids = np.arange(self.size).reshape(self.shape)

    def here(self):
        row, col = lax.axis_index("row"), lax.axis_index("col")
        c, x = self.n["c"], self.n["x"]
        return {"y": row // c, "c": row % c, "z": col // x, "x": col % x}

    def shift(self, value, dim, by):
        to = np.roll(self.ids, -by, axis=list(self.n).index(dim))
        return lax.ppermute(value, AXES, list(zip(self.ids.ravel(), to.ravel())))

    def spread(self, value, dim):
        return [self.shift(value, dim, s) for s in range(1, self.n[dim])]

    def take(self, chunks, dim, by=0):
        at = (self.here()[dim] + by) % self.n[dim]
        return lax.dynamic_index_in_dim(chunks, at, list(self.n).index(dim), keepdims=True)

    def sends(self, chunks, dim):
        return [self.take(chunks, dim, s) for s in range(1, self.n[dim])]

    def reduce(self, chunks, dim, sends=None):
        total = self.take(chunks, dim)
        for s, part in enumerate(sends or self.sends(chunks, dim), 1):
            total = total + self.shift(part, dim, s).astype(f32)
        return total

    def exchange(self, parts):
        return lax.all_to_all(parts, AXES, 0, 0, tiled=True)

    def everywhere(self, part):
        return self.exchange(jnp.broadcast_to(part[None], (self.size,) + part.shape))


ALIGN = 16


def own_rows_kernel(slots, points, factor, out, pbuf, fbuf, psem, fsem):
    cap = out.shape[0]
    width = points.shape[1]

    def copies(i):
        base = pl.multiple_of((slots[0, i] // ALIGN) * ALIGN, ALIGN)
        return (
            pltpu.make_async_copy(
                points.at[pl.ds(base, ALIGN), :], pbuf.at[pl.ds(i * ALIGN, ALIGN), :], psem.at[i]
            ),
            pltpu.make_async_copy(
                factor.at[pl.ds(base, ALIGN), :], fbuf.at[pl.ds(i * ALIGN, ALIGN), :], fsem.at[i]
            ),
        )

    for i in range(cap):
        for copy in copies(i):
            copy.start()
    r = lax.broadcasted_iota(jnp.int32, (cap, cap * ALIGN), 0)
    q = lax.broadcasted_iota(jnp.int32, (cap, cap * ALIGN), 1)
    target = jnp.full((cap, cap * ALIGN), -1, jnp.int32)
    for i in range(cap):
        target = jnp.where(r == i, slots[0, i] % ALIGN + i * ALIGN, target)
    pick = (q == target).astype(f32).astype(bf16)
    for i in range(cap):
        for copy in copies(i):
            copy.wait()
    rows = dot(pick, pbuf[...]).astype(bf16)
    out[:, :width] = normalize(rows)
    out[:, width:] = dot(pick, fbuf[...]).astype(bf16)


def own_rows(points, factor, slots):
    cap = slots.shape[1]
    wide = points.shape[1] + factor.shape[1]
    return pl.pallas_call(
        own_rows_kernel,
        out_shape=jax.ShapeDtypeStruct((cap, wide), bf16),
        in_specs=[pl.BlockSpec(memory_space=pltpu.SMEM), ANY, ANY],
        out_specs=VMEM,
        scratch_shapes=[
            pltpu.VMEM((cap * ALIGN, points.shape[1]), bf16),
            pltpu.VMEM((cap * ALIGN, factor.shape[1]), bf16),
            pltpu.SemaphoreType.DMA((cap,)),
            pltpu.SemaphoreType.DMA((cap,)),
        ],
        cost_estimate=pl.CostEstimate(flops=10**8, bytes_accessed=3 * 10**6, transcendentals=0),
    )(slots, points, factor)


def prepare_kernel(count, width, *refs):
    place, pieces = refs[0], refs[1 : 1 + count]
    turned_ref, ridged_ref, rows, sems = refs[1 + count :]
    copies, at = [], 0
    for k, piece in enumerate(pieces):
        n = piece.shape[0]
        copies.append(pltpu.make_async_copy(piece, rows.at[pl.ds(at, n), :], sems.at[k]))
        at += n
    for copy in copies:
        copy.start()
    slot = lax.broadcasted_iota(jnp.int32, (BLOCK, at), 0)
    pick = (slot == place[...]).astype(f32).astype(bf16)
    for copy in copies:
        copy.wait()
    inter = cosine = None
    for lo in range(0, rows.shape[1], width):
        part = dot(pick, rows[:, lo : lo + width]).astype(bf16)
        turned = part.T
        turned_ref[lo : lo + width, :] = turned
        product = dot(part, turned)
        if lo == 0:
            cosine = product / width
        else:
            inter = product if inter is None else inter + product
    shift = ridge_shift + jnp.max(jnp.sum(jnp.abs(inter), axis=1, keepdims=True))
    r = lax.broadcasted_iota(jnp.int32, (BLOCK, BLOCK), 0)
    c = lax.broadcasted_iota(jnp.int32, (BLOCK, BLOCK), 1)
    ridged_ref[...] = jnp.exp(sharpness * (cosine - 1.0)) - inter + jnp.where(r == c, shift, 0.0)


def prepare(place, pieces, width):
    wide = pieces[0].shape[1]
    total = sum(p.shape[0] for p in pieces)
    return pl.pallas_call(
        functools.partial(prepare_kernel, len(pieces), width),
        out_shape=(
            jax.ShapeDtypeStruct((wide, BLOCK), bf16),
            jax.ShapeDtypeStruct((BLOCK, BLOCK), f32),
        ),
        in_specs=[VMEM] + [ANY] * len(pieces),
        out_specs=(VMEM,) * 2,
        scratch_shapes=[
            pltpu.VMEM((total, wide), bf16),
            pltpu.SemaphoreType.DMA((len(pieces),)),
        ],
        cost_estimate=pl.CostEstimate(
            flops=6 * 10**9, bytes_accessed=10**7, transcendentals=BLOCK * BLOCK
        ),
    )(place, *pieces)


def downdate_kernel(turned, points, factor, targets, high_ref, low_ref, z_ref):
    step = pl.program_id(0)
    width = points.shape[1]
    cosine = dot(normalize(points[...]), turned[:width, :]) / width
    down = jnp.exp(sharpness * (cosine - 1.0)) - dot(factor[...], turned[width:, :])
    high, low = split(down)
    high_ref[...] = high
    low_ref[...] = low
    t = targets[...].T
    part = dot(jnp.concatenate([t, t], 1), jnp.concatenate([high, low], 0))

    @pl.when(step == 0)
    def _():
        z_ref[...] = part

    @pl.when(step > 0)
    def _():
        z_ref[...] += part


def downdate(turned, points, factor, targets):
    pts, width, held, nt = points.shape[0], points.shape[1], factor.shape[1], targets.shape[1]
    blk = 512
    return pl.pallas_call(
        downdate_kernel,
        grid=(pts // blk,),
        out_shape=(
            jax.ShapeDtypeStruct((pts, BLOCK), bf16),
            jax.ShapeDtypeStruct((pts, BLOCK), bf16),
            jax.ShapeDtypeStruct((nt, BLOCK), f32),
        ),
        in_specs=[
            pl.BlockSpec((width + held, BLOCK), lambda i: (0, 0)),
            pl.BlockSpec((blk, width), lambda i: (i, 0)),
            pl.BlockSpec((blk, held), lambda i: (i, 0)),
            pl.BlockSpec((blk, nt), lambda i: (i, 0)),
        ],
        out_specs=(
            pl.BlockSpec((blk, BLOCK), lambda i: (i, 0)),
            pl.BlockSpec((blk, BLOCK), lambda i: (i, 0)),
            pl.BlockSpec((nt, BLOCK), lambda i: (0, 0)),
        ),
        cost_estimate=pl.CostEstimate(
            flops=6 * 10**9, bytes_accessed=16 * 10**6, transcendentals=BLOCK * pts
        ),
    )(turned, points, factor, targets)


def across(v):
    return jnp.broadcast_to(v, (8, TILE))


def base8(tile, lane0):
    e = [[None] * 8 for _ in range(8)]
    for s in range(8):
        col = across(tile[:, lane0 + s : lane0 + s + 1])
        for t in range(s, 8):
            e[t][s] = across(col[t : t + 1, :])
    x = [[None] * 8 for _ in range(8)]
    low = [[None] * 8 for _ in range(8)]
    for s in range(8):
        r = lax.rsqrt(e[s][s])
        for t in range(s + 1, 8):
            low[t][s] = e[t][s] * r
        for u in range(s + 1, 8):
            for t in range(u, 8):
                e[t][u] = e[t][u] - low[t][s] * low[u][s]
        for c in range(s):
            acc = low[s][c] * x[c][c]
            for u in range(c + 1, s):
                acc = acc + low[s][u] * x[u][c]
            x[s][c] = -(r * acc)
        x[s][s] = r
    return x


def columns(x, rowid):
    out = []
    for s in range(8):
        c = jnp.where(rowid == s, x[s][s], 0.0)
        for t in range(s + 1, 8):
            c = jnp.where(rowid == t, x[t][s], c)
        out.append(c)
    return out


def diagonal_block(s_ref, w_ref):
    n, group = TILE, 32
    rowid = lax.broadcasted_iota(jnp.int32, (8, n), 0)
    ri = lax.broadcasted_iota(jnp.int32, (n, n), 0)
    ci = lax.broadcasted_iota(jnp.int32, (n, n), 1)
    w_ref[...] = jnp.where(ri == ci, 1.0, 0.0).astype(f32)
    for g in range(0, n, group):
        tiles = [s_ref[g + 8 * i : g + 8 * i + 8, :] for i in range(4)]
        sides = [w_ref[g + 8 * i : g + 8 * i + 8, :] for i in range(4)]
        for j in range(4):
            lane0 = g + 8 * j
            x = base8(tiles[j], lane0)
            cols = columns(x, rowid)
            u = cols[0] * across(tiles[j][0:1, :])
            q = cols[0] * across(sides[j][0:1, :])
            for s in range(1, 8):
                u = u + cols[s] * across(tiles[j][s : s + 1, :])
                q = q + cols[s] * across(sides[j][s : s + 1, :])
            tiles[j], sides[j] = u, q
            for i in range(j + 1, 4):
                b = [across(tiles[i][:, lane0 + k : lane0 + k + 1]) for k in range(8)]
                t, v = tiles[i], sides[i]
                for s in range(8):
                    m = x[s][0] * b[0]
                    for k in range(1, s + 1):
                        m = m + x[s][k] * b[k]
                    t = t - m * across(u[s : s + 1, :])
                    v = v - m * across(q[s : s + 1, :])
                tiles[i], sides[i] = t, v
        ug = jnp.concatenate(tiles, 0)
        vg = jnp.concatenate(sides, 0)
        w_ref[g : g + group, :] = vg
        if g + group < n:
            lo = g + group
            upd = dot(ug, jnp.concatenate([ug, vg], 1), 0, 0, exact=True)
            s_ref[lo:, :] = s_ref[lo:, :] - upd[lo:, :n]
            w_ref[lo:, :] = w_ref[lo:, :] - upd[lo:, n:]


def factor_kernel(first, last, a_in, r_in, a_ref, r_ref, s_ref, w_ref):
    n, blocks = TILE, BLOCK // TILE
    a_ref[...] = a_in[...]
    r_ref[...] = r_in[...]
    for k in range(first, last):
        o = n * k
        s_ref[...] = a_ref[o : o + n, o : o + n]
        diagonal_block(s_ref, w_ref)
        inv = w_ref[...]
        if k:
            r_ref[o : o + n, :o] = dot(inv, r_ref[o : o + n, :o], exact=True)
        r_ref[o : o + n, o : o + n] = inv
        if k < blocks - 1:
            u = dot(inv, a_ref[o : o + n, o + n :], exact=True)
            wk = r_ref[o : o + n, : o + n]
            a_ref[o + n :, o + n :] = a_ref[o + n :, o + n :] - dot(u, u, 0, 0, exact=True)
            r_ref[o + n :, : o + n] = r_ref[o + n :, : o + n] - dot(u, wk, 0, 0, exact=True)


def factor_step(a, r, first, last):
    return pl.pallas_call(
        functools.partial(factor_kernel, first, last),
        out_shape=(jax.ShapeDtypeStruct(a.shape, f32),) * 2,
        in_specs=[VMEM] * 2,
        out_specs=(VMEM,) * 2,
        scratch_shapes=[pltpu.VMEM((TILE, TILE), f32)] * 2,
        input_output_aliases={0: 0, 1: 1},
        cost_estimate=pl.CostEstimate(
            flops=12 * 10**9, bytes_accessed=4 * 10**6, transcendentals=0
        ),
    )(a, r)


def columns_kernel(inv, high, low, new_ref, turned_ref, norm_ref, acc, left, right):
    step = pl.program_id(0)
    half = BLOCK // 2

    @pl.when(step == 0)
    def _():
        ih, il = split(inv[...].T)
        left[...] = jnp.concatenate([ih[:half, :half], ih[:half, :half], il[:half, :half]], 0)
        right[...] = jnp.concatenate([ih[:, half:], ih[:, half:], il[:, half:]], 0)
        acc[...] = jnp.zeros_like(acc)

    h, l = high[...], low[...]
    for lo, weights in ((0, left), (half, right)):
        k = lo + half
        rows = jnp.concatenate([h[:, :k], l[:, :k], h[:, :k]], 1)
        new = dot(rows, weights[...]).astype(bf16)
        turned_ref[:, lo:k] = new
        new_ref[lo:k, :] = new.T
        wide = new.astype(f32)
        acc[:, lo:k] += jnp.sum((wide * wide).reshape(-1, 8, half), axis=0)

    @pl.when(step == pl.num_programs(0) - 1)
    def _():
        norm_ref[...] = jnp.sum(acc[...], axis=0, keepdims=True)


def make_columns(inv, high, low):
    pts, blk = high.shape[0], 512
    return pl.pallas_call(
        columns_kernel,
        grid=(pts // blk,),
        out_shape=(
            jax.ShapeDtypeStruct((BLOCK, pts), bf16),
            jax.ShapeDtypeStruct((pts, BLOCK), bf16),
            jax.ShapeDtypeStruct((1, BLOCK), f32),
        ),
        in_specs=[
            pl.BlockSpec((BLOCK, BLOCK), lambda i: (0, 0)),
            pl.BlockSpec((blk, BLOCK), lambda i: (i, 0)),
            pl.BlockSpec((blk, BLOCK), lambda i: (i, 0)),
        ],
        out_specs=(
            pl.BlockSpec((BLOCK, blk), lambda i: (0, i)),
            pl.BlockSpec((blk, BLOCK), lambda i: (i, 0)),
            pl.BlockSpec((1, BLOCK), lambda i: (0, 0)),
        ),
        scratch_shapes=[
            pltpu.VMEM((8, BLOCK), f32),
            pltpu.VMEM((3 * BLOCK // 2, BLOCK // 2), bf16),
            pltpu.VMEM((3 * BLOCK, BLOCK // 2), bf16),
        ],
        cost_estimate=pl.CostEstimate(
            flops=4 * 10**9, bytes_accessed=8 * 10**6, transcendentals=0
        ),
    )(inv, high, low)


def on_device(grid, points, factor, targets, pivot_slots, pivot_counts):
    n, me = grid.n, grid.here()
    cap, devices = pivot_slots.shape[1], grid.size
    held, nt, width = factor.shape[1], targets.shape[1], points.shape[1]

    own = own_rows(points, factor, pivot_slots)
    own, late_factor = lax.optimization_barrier((own, factor))
    cross = dot(late_factor, targets, 0, 0)
    squares = jnp.sum(jnp.square(late_factor.astype(f32)), axis=0)
    m = held // devices
    extra = 8 * -(-m // (8 * nt))
    chunks = jnp.concatenate(
        [
            cross.reshape(devices, m, nt),
            jnp.pad(squares.reshape(devices, m), ((0, 0), (0, extra * nt - m))).reshape(
                devices, extra, nt
            ),
        ],
        axis=1,
    )
    chunks = grid.reduce(chunks.reshape(grid.shape + chunks.shape[1:]), "c")

    arrived = grid.spread(own, "z")
    along_z = jnp.concatenate([own] + arrived, 0)
    zs = [(0, 0, s, 0) for s in range(n["z"])]

    def moved(origin, dim, s):
        at = "yczx".index(dim)
        return [tuple(v + s if k == at else v for k, v in enumerate(o)) for o in origin]

    pieces, origins = [along_z], list(zs)
    by_x, by_y = grid.spread(along_z, "x"), grid.spread(along_z, "y")
    pieces += by_x + by_y
    for s in range(1, n["x"]):
        origins += moved(zs, "x", s)
    for s in range(1, n["y"]):
        origins += moved(zs, "y", s)
    for dim in "zxy":
        sends = [part.astype(bf16) for part in grid.sends(chunks, dim)]
        chunks = grid.reduce(chunks, dim, sends)
    half = (n["z"] + 1) // 2
    for s, block in enumerate(by_x, 1):
        pieces += grid.spread(block[: half * cap], "y")
        for r in range(1, n["y"]):
            origins += moved(moved(zs[:half], "x", s), "y", r)
    for r, block in enumerate(by_y, 1):
        if half < n["z"]:
            pieces += grid.spread(block[half * cap :], "x")
            for s in range(1, n["x"]):
                origins += moved(moved(zs[half:], "x", s), "y", r)
    mine, mine_origins = list(pieces), list(origins)
    for s in range(1, n["c"]):
        pieces += [grid.shift(p, "c", s) for p in mine]
        origins += moved(mine_origins, "c", s)

    shifts = np.array(origins)
    dev = jnp.zeros((len(origins),), jnp.int32)
    for k, dim in enumerate("yczx"):
        dev = dev * n[dim] + (me[dim] - shifts[:, k]) % n[dim]
    ends = jnp.cumsum(pivot_counts)
    onehot = dev[:, None] == jnp.arange(devices, dtype=jnp.int32)[None, :]
    count = jnp.sum(jnp.where(onehot, pivot_counts[None, :], 0), axis=1)
    start = jnp.sum(jnp.where(onehot, (ends - pivot_counts)[None, :], 0), axis=1)
    slot = jnp.arange(cap, dtype=jnp.int32)[None, :]
    place = jnp.where(slot < count[:, None], start[:, None] + slot, -1).reshape(1, -1)

    chunks = chunks.reshape(m + extra, nt)
    norm = chunks[m:].reshape(-1)[:m]
    coef = (chunks[:m] / (norm + damping)[:, None]).astype(bf16)
    coef = jnp.broadcast_to(coef[None], (devices,) + coef.shape)

    coef_held = grid.exchange(coef)

    turned, ridged = prepare(place, pieces, width)
    high, low, z = downdate(turned, points, factor, targets)
    z, coef_held = lax.optimization_barrier((z, coef_held))
    coef_held = coef_held.reshape(held, nt)
    t = nt // devices
    z_parts = grid.exchange(z.reshape(devices, t, BLOCK))
    z_own = jnp.sum(z_parts, axis=0)

    inverse = jnp.zeros((BLOCK, BLOCK), f32)
    middle = BLOCK // TILE // 2
    ridged, inverse = factor_step(ridged, inverse, 0, middle)
    ridged, inverse = factor_step(ridged, inverse, middle, BLOCK // TILE)

    new_columns, new_turned, norm_own = make_columns(inverse, high, low)
    cross_own = dot(z_own, inverse, 1, 1, exact=True)
    nh, nl = split(norm_own)
    nl2 = (norm_own - nh.astype(f32) - nl.astype(f32)).astype(bf16)
    late = jnp.concatenate([cross_own.astype(bf16), nh, nl, nl2], axis=0)
    late = jnp.pad(late, ((0, -late.shape[0] % 16), (0, 0)))
    every = grid.everywhere(late).astype(f32)
    norm_new = jnp.sum(every[:, t : t + 3], axis=(0, 1))
    coef_new = (every[:, :t].reshape(nt, BLOCK) / (norm_new + damping)[None, :]).astype(bf16)

    fitted = dot(factor, coef_held)
    return new_columns, (targets.astype(f32) - fitted) - dot(new_turned, coef_new, 1, 1)


def step(grid, *args):
    return on_device(grid, *args)


def solution(mesh):
    spec = P(AXES, None)
    return jax.shard_map(
        functools.partial(step, Grid(mesh)),
        mesh=mesh,
        in_specs=(spec, spec, spec, spec, P()),
        out_specs=(P(None, AXES), spec),
        check_vma=False,
    )
```

```python
import functools

import jax
import jax.numpy as jnp
import numpy as np
from jax import lax
from jax.experimental import pallas as pl
from jax.experimental.pallas import tpu as pltpu
from jax.sharding import PartitionSpec as P

BLOCK = 512
TILE = 128


sharpness = 1.0
ridge_shift = 0.01
damping = 1.0
epsilon = 1e-06

f32 = jnp.float32
bf16 = jnp.bfloat16
AXES = ("row", "col")
VMEM = pl.BlockSpec(memory_space=pltpu.VMEM)
ANY = pl.BlockSpec(memory_space=pl.ANY)


def dot(a, b, da=1, db=0, exact=False):
    return lax.dot_general(
        a,
        b,
        (((da,), (db,)), ((), ())),
        precision=lax.Precision.HIGHEST if exact else None,
        preferred_element_type=f32,
    )


def split(v):
    high = v.astype(bf16)
    return high, (v - high.astype(f32)).astype(bf16)


def normalize(points):
    values = points.astype(f32)
    scale = lax.rsqrt(jnp.mean(values * values, axis=1, keepdims=True) + epsilon)
    return (values * scale).astype(bf16)


class Grid:
    def __init__(self, mesh):
        rows, cols = mesh.shape["row"], mesh.shape["col"]
        c = 2 if rows % 2 == 0 else 1
        x = max(k for k in range(1, cols + 1) if cols % k == 0 and k * k <= cols)
        self.n = {"y": rows // c, "c": c, "z": cols // x, "x": x}
        self.shape = tuple(self.n.values())
        self.size = rows * cols
        self.ids = np.arange(self.size).reshape(self.shape)

    def here(self):
        row, col = lax.axis_index("row"), lax.axis_index("col")
        c, x = self.n["c"], self.n["x"]
        return {"y": row // c, "c": row % c, "z": col // x, "x": col % x}

    def shift(self, value, dim, by):
        to = np.roll(self.ids, -by, axis=list(self.n).index(dim))
        return lax.ppermute(value, AXES, list(zip(self.ids.ravel(), to.ravel())))

    def spread(self, value, dim):
        return [self.shift(value, dim, s) for s in range(1, self.n[dim])]

    def take(self, chunks, dim, by=0):
        at = (self.here()[dim] + by) % self.n[dim]
        return lax.dynamic_index_in_dim(chunks, at, list(self.n).index(dim), keepdims=True)

    def sends(self, chunks, dim):
        return [self.take(chunks, dim, s) for s in range(1, self.n[dim])]

    def reduce(self, chunks, dim, sends=None):
        total = self.take(chunks, dim)
        for s, part in enumerate(sends or self.sends(chunks, dim), 1):
            total = total + self.shift(part, dim, s).astype(f32)
        return total

    def exchange(self, parts):
        return lax.all_to_all(parts, AXES, 0, 0, tiled=True)

    def everywhere(self, part):
        return self.exchange(jnp.broadcast_to(part[None], (self.size,) + part.shape))


ALIGN = 16


def own_rows_kernel(slots, points, factor, out, pbuf, fbuf, psem, fsem):
    cap = out.shape[0]
    width = points.shape[1]

    def copies(i):
        base = pl.multiple_of((slots[0, i] // ALIGN) * ALIGN, ALIGN)
        return (
            pltpu.make_async_copy(
                points.at[pl.ds(base, ALIGN), :], pbuf.at[pl.ds(i * ALIGN, ALIGN), :], psem.at[i]
            ),
            pltpu.make_async_copy(
                factor.at[pl.ds(base, ALIGN), :], fbuf.at[pl.ds(i * ALIGN, ALIGN), :], fsem.at[i]
            ),
        )

    for i in range(cap):
        for copy in copies(i):
            copy.start()
    r = lax.broadcasted_iota(jnp.int32, (cap, cap * ALIGN), 0)
    q = lax.broadcasted_iota(jnp.int32, (cap, cap * ALIGN), 1)
    target = jnp.full((cap, cap * ALIGN), -1, jnp.int32)
    for i in range(cap):
        target = jnp.where(r == i, slots[0, i] % ALIGN + i * ALIGN, target)
    pick = (q == target).astype(f32).astype(bf16)
    for i in range(cap):
        for copy in copies(i):
            copy.wait()
    rows = dot(pick, pbuf[...]).astype(bf16)
    out[:, :width] = normalize(rows)
    out[:, width:] = dot(pick, fbuf[...]).astype(bf16)


def own_rows(points, factor, slots):
    cap = slots.shape[1]
    wide = points.shape[1] + factor.shape[1]
    return pl.pallas_call(
        own_rows_kernel,
        out_shape=jax.ShapeDtypeStruct((cap, wide), bf16),
        in_specs=[pl.BlockSpec(memory_space=pltpu.SMEM), ANY, ANY],
        out_specs=VMEM,
        scratch_shapes=[
            pltpu.VMEM((cap * ALIGN, points.shape[1]), bf16),
            pltpu.VMEM((cap * ALIGN, factor.shape[1]), bf16),
            pltpu.SemaphoreType.DMA((cap,)),
            pltpu.SemaphoreType.DMA((cap,)),
        ],
        cost_estimate=pl.CostEstimate(flops=10**8, bytes_accessed=3 * 10**6, transcendentals=0),
    )(slots, points, factor)


def prepare_kernel(count, width, *refs):
    place, pieces = refs[0], refs[1 : 1 + count]
    turned_ref, ridged_ref, rows, straight, sems = refs[1 + count :]
    copies, at = [], 0
    for k, piece in enumerate(pieces):
        n = piece.shape[0]
        copies.append(pltpu.make_async_copy(piece, rows.at[pl.ds(at, n), :], sems.at[k]))
        at += n
    for copy in copies:
        copy.start()
    slot = lax.broadcasted_iota(jnp.int32, (BLOCK, at), 0)
    pick = (slot == place[...]).astype(f32).astype(bf16)
    for copy in copies:
        copy.wait()
    for lo in range(0, rows.shape[1], width):
        part = dot(pick, rows[:, lo : lo + width]).astype(bf16)
        straight[:, lo : lo + width] = part
        turned_ref[lo : lo + width, :] = part.T
    inter = dot(straight[:, width:], turned_ref[width:, :])
    cosine = dot(straight[:, :width], turned_ref[:width, :]) / width
    shift = ridge_shift + jnp.max(jnp.sum(jnp.abs(inter), axis=1, keepdims=True))
    r = lax.broadcasted_iota(jnp.int32, (BLOCK, BLOCK), 0)
    c = lax.broadcasted_iota(jnp.int32, (BLOCK, BLOCK), 1)
    ridged_ref[...] = jnp.exp(sharpness * (cosine - 1.0)) - inter + jnp.where(r == c, shift, 0.0)


def prepare(place, pieces, width):
    wide = pieces[0].shape[1]
    total = sum(p.shape[0] for p in pieces)
    return pl.pallas_call(
        functools.partial(prepare_kernel, len(pieces), width),
        out_shape=(
            jax.ShapeDtypeStruct((wide, BLOCK), bf16),
            jax.ShapeDtypeStruct((BLOCK, BLOCK), f32),
        ),
        in_specs=[VMEM] + [ANY] * len(pieces),
        out_specs=(VMEM,) * 2,
        scratch_shapes=[
            pltpu.VMEM((total, wide), bf16),
            pltpu.VMEM((BLOCK, wide), bf16),
            pltpu.SemaphoreType.DMA((len(pieces),)),
        ],
        cost_estimate=pl.CostEstimate(
            flops=6 * 10**9, bytes_accessed=10**7, transcendentals=BLOCK * BLOCK
        ),
    )(place, *pieces)


def downdate_kernel(turned, points, factor, targets, high_ref, low_ref, z_ref):
    step = pl.program_id(0)
    width = points.shape[1]
    cosine = dot(normalize(points[...]), turned[:width, :]) / width
    down = jnp.exp(sharpness * (cosine - 1.0)) - dot(factor[...], turned[width:, :])
    high, low = split(down)
    high_ref[...] = high
    low_ref[...] = low
    t = targets[...].T
    part = dot(jnp.concatenate([t, t], 1), jnp.concatenate([high, low], 0))

    @pl.when(step == 0)
    def _():
        z_ref[...] = part

    @pl.when(step > 0)
    def _():
        z_ref[...] += part


def downdate(turned, points, factor, targets):
    pts, width, held, nt = points.shape[0], points.shape[1], factor.shape[1], targets.shape[1]
    blk = 512
    return pl.pallas_call(
        downdate_kernel,
        grid=(pts // blk,),
        out_shape=(
            jax.ShapeDtypeStruct((pts, BLOCK), bf16),
            jax.ShapeDtypeStruct((pts, BLOCK), bf16),
            jax.ShapeDtypeStruct((nt, BLOCK), f32),
        ),
        in_specs=[
            pl.BlockSpec((width + held, BLOCK), lambda i: (0, 0)),
            pl.BlockSpec((blk, width), lambda i: (i, 0)),
            pl.BlockSpec((blk, held), lambda i: (i, 0)),
            pl.BlockSpec((blk, nt), lambda i: (i, 0)),
        ],
        out_specs=(
            pl.BlockSpec((blk, BLOCK), lambda i: (i, 0)),
            pl.BlockSpec((blk, BLOCK), lambda i: (i, 0)),
            pl.BlockSpec((nt, BLOCK), lambda i: (0, 0)),
        ),
        cost_estimate=pl.CostEstimate(
            flops=6 * 10**9, bytes_accessed=16 * 10**6, transcendentals=BLOCK * pts
        ),
    )(turned, points, factor, targets)


def across(v):
    return jnp.broadcast_to(v, (8, TILE))


def base8(tile, lane0):
    e = [[None] * 8 for _ in range(8)]
    for s in range(8):
        col = across(tile[:, lane0 + s : lane0 + s + 1])
        for t in range(s, 8):
            e[t][s] = across(col[t : t + 1, :])
    x = [[None] * 8 for _ in range(8)]
    low = [[None] * 8 for _ in range(8)]
    for s in range(8):
        r = lax.rsqrt(e[s][s])
        for t in range(s + 1, 8):
            low[t][s] = e[t][s] * r
        for u in range(s + 1, 8):
            for t in range(u, 8):
                e[t][u] = e[t][u] - low[t][s] * low[u][s]
        for c in range(s):
            acc = low[s][c] * x[c][c]
            for u in range(c + 1, s):
                acc = acc + low[s][u] * x[u][c]
            x[s][c] = -(r * acc)
        x[s][s] = r
    return x


def columns(x, rowid):
    out = []
    for s in range(8):
        c = jnp.where(rowid == s, x[s][s], 0.0)
        for t in range(s + 1, 8):
            c = jnp.where(rowid == t, x[t][s], c)
        out.append(c)
    return out


def diagonal_block(s_ref, w_ref):
    n, group = TILE, 32
    rowid = lax.broadcasted_iota(jnp.int32, (8, n), 0)
    ri = lax.broadcasted_iota(jnp.int32, (n, n), 0)
    ci = lax.broadcasted_iota(jnp.int32, (n, n), 1)
    w_ref[...] = jnp.where(ri == ci, 1.0, 0.0).astype(f32)
    for g in range(0, n, group):
        tiles = [s_ref[g + 8 * i : g + 8 * i + 8, :] for i in range(4)]
        sides = [w_ref[g + 8 * i : g + 8 * i + 8, :] for i in range(4)]
        for j in range(4):
            lane0 = g + 8 * j
            x = base8(tiles[j], lane0)
            cols = columns(x, rowid)
            u = cols[0] * across(tiles[j][0:1, :])
            q = cols[0] * across(sides[j][0:1, :])
            for s in range(1, 8):
                u = u + cols[s] * across(tiles[j][s : s + 1, :])
                q = q + cols[s] * across(sides[j][s : s + 1, :])
            tiles[j], sides[j] = u, q
            for i in range(j + 1, 4):
                b = [across(tiles[i][:, lane0 + k : lane0 + k + 1]) for k in range(8)]
                t, v = tiles[i], sides[i]
                for s in range(8):
                    m = x[s][0] * b[0]
                    for k in range(1, s + 1):
                        m = m + x[s][k] * b[k]
                    t = t - m * across(u[s : s + 1, :])
                    v = v - m * across(q[s : s + 1, :])
                tiles[i], sides[i] = t, v
        ug = jnp.concatenate(tiles, 0)
        vg = jnp.concatenate(sides, 0)
        w_ref[g : g + group, :] = vg
        if g + group < n:
            lo = g + group
            upd = dot(ug, jnp.concatenate([ug, vg], 1), 0, 0, exact=True)
            s_ref[lo:, :] = s_ref[lo:, :] - upd[lo:, :n]
            w_ref[lo:, :] = w_ref[lo:, :] - upd[lo:, n:]


def factor_kernel(first, last, a_in, r_in, a_ref, r_ref, s_ref, w_ref):
    n, blocks = TILE, BLOCK // TILE
    a_ref[...] = a_in[...]
    r_ref[...] = r_in[...]
    for k in range(first, last):
        o = n * k
        s_ref[...] = a_ref[o : o + n, o : o + n]
        diagonal_block(s_ref, w_ref)
        inv = w_ref[...]
        if k:
            r_ref[o : o + n, :o] = dot(inv, r_ref[o : o + n, :o], exact=True)
        r_ref[o : o + n, o : o + n] = inv
        if k < blocks - 1:
            u = dot(inv, a_ref[o : o + n, o + n :], exact=True)
            wk = r_ref[o : o + n, : o + n]
            a_ref[o + n :, o + n :] = a_ref[o + n :, o + n :] - dot(u, u, 0, 0, exact=True)
            r_ref[o + n :, : o + n] = r_ref[o + n :, : o + n] - dot(u, wk, 0, 0, exact=True)


def factor_step(a, r, first, last):
    return pl.pallas_call(
        functools.partial(factor_kernel, first, last),
        out_shape=(jax.ShapeDtypeStruct(a.shape, f32),) * 2,
        in_specs=[VMEM] * 2,
        out_specs=(VMEM,) * 2,
        scratch_shapes=[pltpu.VMEM((TILE, TILE), f32)] * 2,
        input_output_aliases={0: 0, 1: 1},
        cost_estimate=pl.CostEstimate(
            flops=12 * 10**9, bytes_accessed=4 * 10**6, transcendentals=0
        ),
    )(a, r)


def columns_kernel(inv, high, low, new_ref, turned_ref, norm_ref, acc, left, right):
    step = pl.program_id(0)
    half = BLOCK // 2

    @pl.when(step == 0)
    def _():
        ih, il = split(inv[...].T)
        left[...] = jnp.concatenate([ih[:half, :half], ih[:half, :half], il[:half, :half]], 0)
        right[...] = jnp.concatenate([ih[:, half:], ih[:, half:], il[:, half:]], 0)
        acc[...] = jnp.zeros_like(acc)

    h, l = high[...], low[...]
    for lo, weights in ((0, left), (half, right)):
        k = lo + half
        rows = jnp.concatenate([h[:, :k], l[:, :k], h[:, :k]], 1)
        new = dot(rows, weights[...]).astype(bf16)
        turned_ref[:, lo:k] = new
        new_ref[lo:k, :] = new.T
        wide = new.astype(f32)
        acc[:, lo:k] += jnp.sum((wide * wide).reshape(-1, 8, half), axis=0)

    @pl.when(step == pl.num_programs(0) - 1)
    def _():
        norm_ref[...] = jnp.sum(acc[...], axis=0, keepdims=True)


def make_columns(inv, high, low):
    pts, blk = high.shape[0], 512
    return pl.pallas_call(
        columns_kernel,
        grid=(pts // blk,),
        out_shape=(
            jax.ShapeDtypeStruct((BLOCK, pts), bf16),
            jax.ShapeDtypeStruct((pts, BLOCK), bf16),
            jax.ShapeDtypeStruct((1, BLOCK), f32),
        ),
        in_specs=[
            pl.BlockSpec((BLOCK, BLOCK), lambda i: (0, 0)),
            pl.BlockSpec((blk, BLOCK), lambda i: (i, 0)),
            pl.BlockSpec((blk, BLOCK), lambda i: (i, 0)),
        ],
        out_specs=(
            pl.BlockSpec((BLOCK, blk), lambda i: (0, i)),
            pl.BlockSpec((blk, BLOCK), lambda i: (i, 0)),
            pl.BlockSpec((1, BLOCK), lambda i: (0, 0)),
        ),
        scratch_shapes=[
            pltpu.VMEM((8, BLOCK), f32),
            pltpu.VMEM((3 * BLOCK // 2, BLOCK // 2), bf16),
            pltpu.VMEM((3 * BLOCK, BLOCK // 2), bf16),
        ],
        cost_estimate=pl.CostEstimate(
            flops=4 * 10**9, bytes_accessed=8 * 10**6, transcendentals=0
        ),
    )(inv, high, low)


def finish_kernel(base, turned, coef, out):
    out[...] = base[...] - dot(turned[...], coef[...], 1, 1)


def finish(base, turned, coef):
    pts, nt = base.shape
    blk = pts // 2
    return pl.pallas_call(
        finish_kernel,
        grid=(pts // blk,),
        out_shape=jax.ShapeDtypeStruct((pts, nt), f32),
        in_specs=[
            pl.BlockSpec((blk, nt), lambda i: (i, 0)),
            pl.BlockSpec((blk, BLOCK), lambda i: (i, 0)),
            pl.BlockSpec((nt, BLOCK), lambda i: (0, 0)),
        ],
        out_specs=pl.BlockSpec((blk, nt), lambda i: (i, 0)),
        cost_estimate=pl.CostEstimate(
            flops=10**9, bytes_accessed=8 * 10**6, transcendentals=0
        ),
    )(base, turned, coef)


def on_device(grid, points, factor, targets, pivot_slots, pivot_counts):
    n, me = grid.n, grid.here()
    cap, devices = pivot_slots.shape[1], grid.size
    held, nt, width = factor.shape[1], targets.shape[1], points.shape[1]

    own = own_rows(points, factor, pivot_slots)
    own, late_factor = lax.optimization_barrier((own, factor))
    cross = dot(late_factor, targets, 0, 0)
    squares = jnp.sum(jnp.square(late_factor.astype(f32)), axis=0)
    m = held // devices
    extra = 8 * -(-m // (8 * nt))
    chunks = jnp.concatenate(
        [
            cross.reshape(devices, m, nt),
            jnp.pad(squares.reshape(devices, m), ((0, 0), (0, extra * nt - m))).reshape(
                devices, extra, nt
            ),
        ],
        axis=1,
    )
    chunks = grid.reduce(chunks.reshape(grid.shape + chunks.shape[1:]), "c")

    def moved(origin, dim, s):
        at = "yczx".index(dim)
        return [tuple(v + s if k == at else v for k, v in enumerate(o)) for o in origin]

    blocks = [own] + grid.spread(own, "z")
    unit = max(1, ALIGN // cap)
    along_z = []
    for k in range(0, n["z"], unit):
        part = blocks[k : k + unit]
        along_z.append(
            (
                part[0] if len(part) == 1 else jnp.concatenate(part, 0),
                [(0, 0, s, 0) for s in range(k, k + len(part))],
            )
        )

    def forward(units, dim):
        return [
            (grid.shift(part, dim, s), moved(origin, dim, s))
            for part, origin in units
            for s in range(1, n[dim])
        ]

    half = (len(along_z) + 1) // 2
    found = list(along_z)
    for k, one in enumerate(along_z):
        by_x, by_y = forward([one], "x"), forward([one], "y")
        both = forward(by_x, "y") if k < half else forward(by_y, "x")
        found += by_x + by_y + both
    found += forward(found, "c")
    pieces = [part for part, _ in found]
    origins = [o for _, origin in found for o in origin]
    for dim in "zxy":
        sends = [part.astype(bf16) for part in grid.sends(chunks, dim)]
        chunks = grid.reduce(chunks, dim, sends)

    shifts = np.array(origins)
    dev = jnp.zeros((len(origins),), jnp.int32)
    for k, dim in enumerate("yczx"):
        dev = dev * n[dim] + (me[dim] - shifts[:, k]) % n[dim]
    ends = jnp.cumsum(pivot_counts)
    onehot = dev[:, None] == jnp.arange(devices, dtype=jnp.int32)[None, :]
    count = jnp.sum(jnp.where(onehot, pivot_counts[None, :], 0), axis=1)
    start = jnp.sum(jnp.where(onehot, (ends - pivot_counts)[None, :], 0), axis=1)
    slot = jnp.arange(cap, dtype=jnp.int32)[None, :]
    place = jnp.where(slot < count[:, None], start[:, None] + slot, -1).reshape(1, -1)

    chunks = chunks.reshape(m + extra, nt)
    norm = chunks[m:].reshape(-1)[:m]
    coef = (chunks[:m] / (norm + damping)[:, None]).astype(bf16)
    coef = jnp.broadcast_to(coef[None], (devices,) + coef.shape)

    coef_held = grid.exchange(coef)

    turned, ridged = prepare(place, pieces, width)
    high, low, z = downdate(turned, points, factor, targets)
    z, coef_held = lax.optimization_barrier((z, coef_held))
    coef_held = coef_held.reshape(held, nt)
    t = nt // devices
    z_parts = grid.exchange(z.reshape(devices, t, BLOCK))
    z_own = jnp.sum(z_parts, axis=0)

    inverse = jnp.zeros((BLOCK, BLOCK), f32)
    middle = BLOCK // TILE // 2
    ridged, inverse = factor_step(ridged, inverse, 0, middle)
    ridged, inverse = factor_step(ridged, inverse, middle, BLOCK // TILE)

    new_columns, new_turned, norm_own = make_columns(inverse, high, low)
    cross_own = dot(z_own, inverse, 1, 1, exact=True)
    nh, nl = split(norm_own)
    nl2 = (norm_own - nh.astype(f32) - nl.astype(f32)).astype(bf16)
    late = jnp.concatenate([cross_own.astype(bf16), nh, nl, nl2], axis=0)
    late = jnp.pad(late, ((0, -late.shape[0] % 16), (0, 0)))
    every = grid.everywhere(late).astype(f32)
    norm_new = jnp.sum(every[:, t : t + 3], axis=(0, 1))
    coef_new = (every[:, :t].reshape(nt, BLOCK) / (norm_new + damping)[None, :]).astype(bf16)

    base = targets.astype(f32) - dot(factor, coef_held)
    return new_columns, finish(base, new_turned, coef_new)


def step(grid, *args):
    return on_device(grid, *args)


def solution(mesh):
    spec = P(AXES, None)
    return jax.shard_map(
        functools.partial(step, Grid(mesh)),
        mesh=mesh,
        in_specs=(spec, spec, spec, spec, P()),
        out_specs=(P(None, AXES), spec),
        check_vma=False,
    )
```

```python
import functools

import jax
import jax.numpy as jnp
import numpy as np
from jax import lax
from jax.experimental import pallas as pl
from jax.experimental.pallas import tpu as pltpu
from jax.sharding import PartitionSpec as P

BLOCK = 512
TILE = 128


sharpness = 1.0
ridge_shift = 0.01
damping = 1.0
epsilon = 1e-06

f32 = jnp.float32
bf16 = jnp.bfloat16
AXES = ("row", "col")
VMEM = pl.BlockSpec(memory_space=pltpu.VMEM)
ANY = pl.BlockSpec(memory_space=pl.ANY)


def dot(a, b, da=1, db=0, exact=False):
    return lax.dot_general(
        a,
        b,
        (((da,), (db,)), ((), ())),
        precision=lax.Precision.HIGHEST if exact else None,
        preferred_element_type=f32,
    )


def split(v):
    high = v.astype(bf16)
    return high, (v - high.astype(f32)).astype(bf16)


def normalize(points):
    values = points.astype(f32)
    scale = lax.rsqrt(jnp.mean(values * values, axis=1, keepdims=True) + epsilon)
    return (values * scale).astype(bf16)


class Grid:
    def __init__(self, mesh):
        rows, cols = mesh.shape["row"], mesh.shape["col"]
        c = 2 if rows % 2 == 0 else 1
        x = max(k for k in range(1, cols + 1) if cols % k == 0 and k * k <= cols)
        self.n = {"y": rows // c, "c": c, "z": cols // x, "x": x}
        self.shape = tuple(self.n.values())
        self.size = rows * cols
        self.ids = np.arange(self.size).reshape(self.shape)

    def here(self):
        row, col = lax.axis_index("row"), lax.axis_index("col")
        c, x = self.n["c"], self.n["x"]
        return {"y": row // c, "c": row % c, "z": col // x, "x": col % x}

    def paired(self, dim):
        return self.n[dim] & (self.n[dim] - 1) == 0

    def source(self, at, dim, by):
        return at ^ by if self.paired(dim) else (at - by) % self.n[dim]

    def shift(self, value, dim, by):
        axis = list(self.n).index(dim)
        if self.paired(dim):
            to = np.take(self.ids, np.arange(self.n[dim]) ^ by, axis=axis)
        else:
            to = np.roll(self.ids, -by, axis=axis)
        return lax.ppermute(value, AXES, list(zip(self.ids.ravel(), to.ravel())))

    def spread(self, value, dim):
        return [self.shift(value, dim, s) for s in range(1, self.n[dim])]

    def take(self, chunks, dim, by=0):
        at = self.here()[dim]
        if by:
            at = at ^ by if self.paired(dim) else (at + by) % self.n[dim]
        return lax.dynamic_index_in_dim(chunks, at, list(self.n).index(dim), keepdims=True)

    def sends(self, chunks, dim):
        return [self.take(chunks, dim, s) for s in range(1, self.n[dim])]

    def reduce(self, chunks, dim, sends=None):
        total = self.take(chunks, dim)
        for s, part in enumerate(sends or self.sends(chunks, dim), 1):
            total = total + self.shift(part, dim, s).astype(f32)
        return total

    def exchange(self, parts):
        return lax.all_to_all(parts, AXES, 0, 0, tiled=True)

    def everywhere(self, part):
        return self.exchange(jnp.broadcast_to(part[None], (self.size,) + part.shape))


ALIGN = 16


def own_rows_kernel(slots, points, factor, out, pbuf, fbuf, psem, fsem):
    cap = out.shape[0]
    width = points.shape[1]

    def copies(i, base):
        return (
            pltpu.make_async_copy(
                points.at[pl.ds(base, ALIGN), :], pbuf.at[pl.ds(i * ALIGN, ALIGN), :], psem.at[i]
            ),
            pltpu.make_async_copy(
                factor.at[pl.ds(base, ALIGN), :], fbuf.at[pl.ds(i * ALIGN, ALIGN), :], fsem.at[i]
            ),
        )

    for i in range(cap):
        for copy in copies(i, pl.multiple_of((slots[0, i] // ALIGN) * ALIGN, ALIGN)):
            copy.start()
    r = lax.broadcasted_iota(jnp.int32, (cap, cap * ALIGN), 0)
    q = lax.broadcasted_iota(jnp.int32, (cap, cap * ALIGN), 1)
    target = jnp.full((cap, cap * ALIGN), -1, jnp.int32)
    for i in range(cap):
        target = jnp.where(r == i, slots[0, i] % ALIGN + i * ALIGN, target)
    pick = (q == target).astype(f32).astype(bf16)
    for i in range(cap):
        for copy in copies(i, 0):
            copy.wait()
    rows = dot(pick, pbuf[...]).astype(bf16)
    out[:, :width] = normalize(rows)
    out[:, width:] = dot(pick, fbuf[...]).astype(bf16)


def own_rows(points, factor, slots):
    cap = slots.shape[1]
    wide = points.shape[1] + factor.shape[1]
    return pl.pallas_call(
        own_rows_kernel,
        out_shape=jax.ShapeDtypeStruct((cap, wide), bf16),
        in_specs=[pl.BlockSpec(memory_space=pltpu.SMEM), ANY, ANY],
        out_specs=VMEM,
        scratch_shapes=[
            pltpu.VMEM((cap * ALIGN, points.shape[1]), bf16),
            pltpu.VMEM((cap * ALIGN, factor.shape[1]), bf16),
            pltpu.SemaphoreType.DMA((cap,)),
            pltpu.SemaphoreType.DMA((cap,)),
        ],
        cost_estimate=pl.CostEstimate(flops=10**8, bytes_accessed=3 * 10**6, transcendentals=0),
    )(slots, points, factor)


def prepare_kernel(count, width, *refs):
    place, pieces = refs[0], refs[1 : 1 + count]
    turned_ref, ridged_ref, rows, straight, sems = refs[1 + count :]
    copies, at = [], 0
    for k, piece in enumerate(pieces):
        n = piece.shape[0]
        copies.append(pltpu.make_async_copy(piece, rows.at[pl.ds(at, n), :], sems.at[k]))
        at += n
    for copy in copies:
        copy.start()
    slot = lax.broadcasted_iota(jnp.int32, (BLOCK, at), 0)
    pick = (slot == place[...]).astype(f32).astype(bf16)
    for copy in copies:
        copy.wait()
    for lo in range(0, rows.shape[1], width):
        part = dot(pick, rows[:, lo : lo + width]).astype(bf16)
        straight[:, lo : lo + width] = part
        turned_ref[lo : lo + width, :] = part.T
    inter = dot(straight[:, width:], turned_ref[width:, :])
    cosine = dot(straight[:, :width], turned_ref[:width, :]) / width
    shift = ridge_shift + jnp.max(jnp.sum(jnp.abs(inter), axis=1, keepdims=True))
    r = lax.broadcasted_iota(jnp.int32, (BLOCK, BLOCK), 0)
    c = lax.broadcasted_iota(jnp.int32, (BLOCK, BLOCK), 1)
    ridged_ref[...] = jnp.exp(sharpness * (cosine - 1.0)) - inter + jnp.where(r == c, shift, 0.0)


def prepare(place, pieces, width):
    wide = pieces[0].shape[1]
    total = sum(p.shape[0] for p in pieces)
    return pl.pallas_call(
        functools.partial(prepare_kernel, len(pieces), width),
        out_shape=(
            jax.ShapeDtypeStruct((wide, BLOCK), bf16),
            jax.ShapeDtypeStruct((BLOCK, BLOCK), f32),
        ),
        in_specs=[VMEM] + [ANY] * len(pieces),
        out_specs=(VMEM,) * 2,
        scratch_shapes=[
            pltpu.VMEM((total, wide), bf16),
            pltpu.VMEM((BLOCK, wide), bf16),
            pltpu.SemaphoreType.DMA((len(pieces),)),
        ],
        cost_estimate=pl.CostEstimate(
            flops=6 * 10**9, bytes_accessed=10**7, transcendentals=BLOCK * BLOCK
        ),
    )(place, *pieces)


def downdate_kernel(turned, points, factor, targets, high_ref, low_ref, z_ref):
    step = pl.program_id(0)
    width = points.shape[1]
    cosine = dot(normalize(points[...]), turned[:width, :]) / width
    down = jnp.exp(sharpness * (cosine - 1.0)) - dot(factor[...], turned[width:, :])
    high, low = split(down)
    high_ref[...] = high
    low_ref[...] = low
    t = targets[...].T
    part = dot(jnp.concatenate([t, t], 1), jnp.concatenate([high, low], 0))

    @pl.when(step == 0)
    def _():
        z_ref[...] = part

    @pl.when(step > 0)
    def _():
        z_ref[...] += part


def downdate(turned, points, factor, targets):
    pts, width, held, nt = points.shape[0], points.shape[1], factor.shape[1], targets.shape[1]
    blk = 512
    return pl.pallas_call(
        downdate_kernel,
        grid=(pts // blk,),
        out_shape=(
            jax.ShapeDtypeStruct((pts, BLOCK), bf16),
            jax.ShapeDtypeStruct((pts, BLOCK), bf16),
            jax.ShapeDtypeStruct((nt, BLOCK), f32),
        ),
        in_specs=[
            pl.BlockSpec((width + held, BLOCK), lambda i: (0, 0)),
            pl.BlockSpec((blk, width), lambda i: (i, 0)),
            pl.BlockSpec((blk, held), lambda i: (i, 0)),
            pl.BlockSpec((blk, nt), lambda i: (i, 0)),
        ],
        out_specs=(
            pl.BlockSpec((blk, BLOCK), lambda i: (i, 0)),
            pl.BlockSpec((blk, BLOCK), lambda i: (i, 0)),
            pl.BlockSpec((nt, BLOCK), lambda i: (0, 0)),
        ),
        cost_estimate=pl.CostEstimate(
            flops=6 * 10**9, bytes_accessed=16 * 10**6, transcendentals=BLOCK * pts
        ),
    )(turned, points, factor, targets)


GROUP = 64


def across(v):
    return jnp.broadcast_to(v, (8, TILE))


def lanes(tile, lane0):
    return [across(tile[:, lane0 + s : lane0 + s + 1]) for s in range(8)]


def eliminate(tile, side, others, lane0, rowid, scratch):
    col = lanes(tile, lane0)
    for s in range(8):
        scratch[8 * s : 8 * s + 8, :] = col[s]
    e = [
        [scratch[pl.ds(8 * s + t, 8, stride=0), :] if t >= s else None for s in range(8)]
        for t in range(8)
    ]
    below = [lanes(t, lane0) for t, _ in others]
    out = [list(o) for o in others]
    scale = None
    for s in range(8):
        r = lax.rsqrt(e[s][s])
        scale = r if s == 0 else jnp.where(rowid == s, r, scale)
        low = [None] * 8
        for t in range(s + 1, 8):
            low[t] = e[t][s] * r
        for u in range(s + 1, 8):
            for t in range(u, 8):
                e[t][u] = e[t][u] - low[t] * low[u]
        row, wide = across(tile[s : s + 1, :]) * r, across(side[s : s + 1, :]) * r
        if s < 7:
            mine = jnp.where(rowid > s, col[s], 0.0) * r
            tile = tile - mine * row
            side = side - mine * wide
            for u in range(s + 1, 8):
                col[u] = col[u] - mine * low[u]
        for k, b in enumerate(below):
            m = b[s] * r
            out[k][0] = out[k][0] - m * row
            out[k][1] = out[k][1] - m * wide
            for u in range(s + 1, 8):
                b[u] = b[u] - m * low[u]
    return tile * scale, side * scale, out


def diagonal_block(s_ref, w_ref, scratch):
    n, count = TILE, GROUP // 8
    rowid = lax.broadcasted_iota(jnp.int32, (8, n), 0)
    ri = lax.broadcasted_iota(jnp.int32, (n, n), 0)
    ci = lax.broadcasted_iota(jnp.int32, (n, n), 1)
    w_ref[...] = jnp.where(ri == ci, 1.0, 0.0).astype(f32)
    for g in range(0, n, GROUP):
        tiles = [s_ref[g + 8 * i : g + 8 * i + 8, :] for i in range(count)]
        sides = [w_ref[g + 8 * i : g + 8 * i + 8, :] for i in range(count)]
        for j in range(count):
            rest = list(zip(tiles[j + 1 :], sides[j + 1 :]))
            tiles[j], sides[j], rest = eliminate(
                tiles[j], sides[j], rest, g + 8 * j, rowid, scratch.at[j % 2]
            )
            tiles[j + 1 :] = [t for t, _ in rest]
            sides[j + 1 :] = [v for _, v in rest]
        ug, vg = jnp.concatenate(tiles, 0), jnp.concatenate(sides, 0)
        w_ref[g : g + GROUP, :] = vg
        if g + GROUP < n:
            lo = g + GROUP
            upd = dot(ug, jnp.concatenate([ug, vg], 1), 0, 0, exact=True)
            s_ref[lo:, :] = s_ref[lo:, :] - upd[lo:, :n]
            w_ref[lo:, :] = w_ref[lo:, :] - upd[lo:, n:]


def factor_kernel(first, last, a_in, r_in, a_ref, r_ref, s_ref, w_ref, scratch):
    n, blocks = TILE, BLOCK // TILE
    mul = functools.partial(dot, exact=True)
    a_ref[...] = a_in[...]
    r_ref[...] = r_in[...]

    def finish(k, inv, u):
        o, p, q = n * k, n * (k + 1), n * (k + 2)
        if k:
            r_ref[o:p, :o] = mul(inv, r_ref[o:p, :o])
        r_ref[o:p, o:p] = inv
        if k < blocks - 1:
            done = r_ref[o:p, :p]
            r_ref[p:q, :p] = r_ref[p:q, :p] - mul(u, done, 0, 0)
            if k < blocks - 2:
                v = mul(inv, a_ref[o:p, q:])
                a_ref[p:q, q:] = a_ref[p:q, q:] - mul(u, v, 0, 0)
                a_ref[q:, q:] = a_ref[q:, q:] - mul(v, v, 0, 0)
                r_ref[q:, :p] = r_ref[q:, :p] - mul(v, done, 0, 0)

    s_ref[first % 2] = a_ref[n * first : n * first + n, n * first : n * first + n]
    if first:
        o, p = n * (first - 1), n * first
        finish(first - 1, r_ref[o:p, o:p], a_ref[o:p, p : p + n])
    for k in range(first, last):
        o, p, q = n * k, n * (k + 1), n * (k + 2)
        w = w_ref.at[k % 2]
        diagonal_block(s_ref.at[k % 2], w, scratch)
        inv, u = w[...], None
        if k < blocks - 1:
            u = mul(inv, a_ref[o:p, p:q])
            ahead = a_ref[p:q, p:q] - mul(u, u, 0, 0)
            if k + 1 < last:
                s_ref[(k + 1) % 2] = ahead
            else:
                a_ref[p:q, p:q] = ahead
                a_ref[o:p, p:q] = u
                r_ref[o:p, o:p] = inv
        if k + 1 < last or k == blocks - 1:
            finish(k, inv, u)


def factor_step(a, r, first, last):
    return pl.pallas_call(
        functools.partial(factor_kernel, first, last),
        out_shape=(jax.ShapeDtypeStruct(a.shape, f32),) * 2,
        in_specs=[VMEM] * 2,
        out_specs=(VMEM,) * 2,
        scratch_shapes=[pltpu.VMEM((2, TILE, TILE), f32)] * 2 + [pltpu.VMEM((2, 64, TILE), f32)],
        input_output_aliases={0: 0, 1: 1},
        cost_estimate=pl.CostEstimate(
            flops=12 * 10**9, bytes_accessed=4 * 10**6, transcendentals=0
        ),
    )(a, r)


def columns_kernel(inv, high, low, new_ref, turned_ref, norm_ref, acc, left, right):
    step = pl.program_id(0)
    half = BLOCK // 2

    @pl.when(step == 0)
    def _():
        ih, il = split(inv[...].T)
        left[...] = jnp.concatenate([ih[:half, :half], ih[:half, :half], il[:half, :half]], 0)
        right[...] = jnp.concatenate([ih[:, half:], ih[:, half:], il[:, half:]], 0)
        acc[...] = jnp.zeros_like(acc)

    h, l = high[...], low[...]
    for lo, weights in ((0, left), (half, right)):
        k = lo + half
        rows = jnp.concatenate([h[:, :k], l[:, :k], h[:, :k]], 1)
        new = dot(rows, weights[...]).astype(bf16)
        turned_ref[:, lo:k] = new
        new_ref[lo:k, :] = new.T
        wide = new.astype(f32)
        acc[:, lo:k] += jnp.sum((wide * wide).reshape(-1, 8, half), axis=0)

    @pl.when(step == pl.num_programs(0) - 1)
    def _():
        norm_ref[...] = jnp.sum(acc[...], axis=0, keepdims=True)


def make_columns(inv, high, low):
    pts, blk = high.shape[0], 512
    return pl.pallas_call(
        columns_kernel,
        grid=(pts // blk,),
        out_shape=(
            jax.ShapeDtypeStruct((BLOCK, pts), bf16),
            jax.ShapeDtypeStruct((pts, BLOCK), bf16),
            jax.ShapeDtypeStruct((1, BLOCK), f32),
        ),
        in_specs=[
            pl.BlockSpec((BLOCK, BLOCK), lambda i: (0, 0)),
            pl.BlockSpec((blk, BLOCK), lambda i: (i, 0)),
            pl.BlockSpec((blk, BLOCK), lambda i: (i, 0)),
        ],
        out_specs=(
            pl.BlockSpec((BLOCK, blk), lambda i: (0, i)),
            pl.BlockSpec((blk, BLOCK), lambda i: (i, 0)),
            pl.BlockSpec((1, BLOCK), lambda i: (0, 0)),
        ),
        scratch_shapes=[
            pltpu.VMEM((8, BLOCK), f32),
            pltpu.VMEM((3 * BLOCK // 2, BLOCK // 2), bf16),
            pltpu.VMEM((3 * BLOCK, BLOCK // 2), bf16),
        ],
        cost_estimate=pl.CostEstimate(
            flops=4 * 10**9, bytes_accessed=8 * 10**6, transcendentals=0
        ),
    )(inv, high, low)


def parcel_kernel(parts, inv, norm, out):
    t = parts.shape[1]
    z = parts[0]
    for k in range(1, parts.shape[0]):
        z = z + parts[k]
    cross = dot(z, inv[...], 1, 1, exact=True)
    n0 = norm[...].astype(bf16).astype(f32)
    n1 = (norm[...] - n0).astype(bf16).astype(f32)
    n2 = norm[...] - n0 - n1
    row = lax.broadcasted_iota(jnp.int32, (out.shape[1], cross.shape[1]), 0)
    own = jnp.concatenate([cross] * (out.shape[1] // t), 0)
    for k, v in enumerate((n0, n1, n2)):
        own = jnp.where(row == t + k, jnp.broadcast_to(v, own.shape), own)
    own = own.astype(bf16)
    for k in range(out.shape[0]):
        out[k] = own


def make_parcel(parts, inv, norm):
    devices, t, block = parts.shape
    rows = t * -(-(-(-(t + 3) // 16) * 16) // t)
    return pl.pallas_call(
        parcel_kernel,
        out_shape=jax.ShapeDtypeStruct((devices, rows, block), bf16),
        in_specs=[VMEM] * 3,
        out_specs=VMEM,
        cost_estimate=pl.CostEstimate(
            flops=10**8, bytes_accessed=2 * 10**6, transcendentals=0
        ),
    )(parts, inv, norm)


def finish_kernel(base, turned, coef, out):
    out[...] = base[...] - dot(turned[...], coef[...], 1, 1)


def finish(base, turned, coef):
    pts, nt = base.shape
    blk = pts // 2
    return pl.pallas_call(
        finish_kernel,
        grid=(pts // blk,),
        out_shape=jax.ShapeDtypeStruct((pts, nt), f32),
        in_specs=[
            pl.BlockSpec((blk, nt), lambda i: (i, 0)),
            pl.BlockSpec((blk, BLOCK), lambda i: (i, 0)),
            pl.BlockSpec((nt, BLOCK), lambda i: (0, 0)),
        ],
        out_specs=pl.BlockSpec((blk, nt), lambda i: (i, 0)),
        cost_estimate=pl.CostEstimate(
            flops=10**9, bytes_accessed=8 * 10**6, transcendentals=0
        ),
    )(base, turned, coef)


def on_device(grid, points, factor, targets, pivot_slots, pivot_counts):
    n, me = grid.n, grid.here()
    cap, devices = pivot_slots.shape[1], grid.size
    held, nt, width = factor.shape[1], targets.shape[1], points.shape[1]

    own = own_rows(points, factor, pivot_slots)
    own, late_factor = lax.optimization_barrier((own, factor))
    cross = dot(late_factor, targets, 0, 0)
    squares = jnp.sum(jnp.square(late_factor.astype(f32)), axis=0)
    m = held // devices
    extra = 8 * -(-m // (8 * nt))
    chunks = jnp.concatenate(
        [
            cross.reshape(devices, m, nt),
            jnp.pad(squares.reshape(devices, m), ((0, 0), (0, extra * nt - m))).reshape(
                devices, extra, nt
            ),
        ],
        axis=1,
    )
    chunks = grid.reduce(chunks.reshape(grid.shape + chunks.shape[1:]), "c")

    def moved(origin, dim, s):
        at = "yczx".index(dim)
        return [tuple(v + s if k == at else v for k, v in enumerate(o)) for o in origin]

    blocks = [own] + grid.spread(own, "z")
    unit = max(1, ALIGN // cap)
    along_z = []
    for k in range(0, n["z"], unit):
        part = blocks[k : k + unit]
        along_z.append(
            (
                part[0] if len(part) == 1 else jnp.concatenate(part, 0),
                [(0, 0, s, 0) for s in range(k, k + len(part))],
            )
        )

    def forward(units, dim):
        return [
            (grid.shift(part, dim, s), moved(origin, dim, s))
            for part, origin in units
            for s in range(1, n[dim])
        ]

    half = (len(along_z) + 1) // 2
    found = list(along_z)
    for k, one in enumerate(along_z):
        by_x, by_y = forward([one], "x"), forward([one], "y")
        both = forward(by_x, "y") if k < half else forward(by_y, "x")
        found += by_x + by_y + both
    found += forward(found, "c")
    pieces = [part for part, _ in found]
    origins = [o for _, origin in found for o in origin]
    for dim in "zxy":
        sends = [part.astype(bf16) for part in grid.sends(chunks, dim)]
        chunks = grid.reduce(chunks, dim, sends)

    shifts = np.array(origins)
    dev = jnp.zeros((len(origins),), jnp.int32)
    for k, dim in enumerate("yczx"):
        dev = dev * n[dim] + grid.source(me[dim], dim, jnp.asarray(shifts[:, k], jnp.int32))
    ends = jnp.cumsum(pivot_counts)
    onehot = dev[:, None] == jnp.arange(devices, dtype=jnp.int32)[None, :]
    count = jnp.sum(jnp.where(onehot, pivot_counts[None, :], 0), axis=1)
    start = jnp.sum(jnp.where(onehot, (ends - pivot_counts)[None, :], 0), axis=1)
    slot = jnp.arange(cap, dtype=jnp.int32)[None, :]
    place = jnp.where(slot < count[:, None], start[:, None] + slot, -1).reshape(1, -1)

    chunks = chunks.reshape(m + extra, nt)
    norm = chunks[m:].reshape(-1)[:m]
    coef = (chunks[:m] / (norm + damping)[:, None]).astype(bf16)
    coef = jnp.broadcast_to(coef[None], (devices,) + coef.shape)

    coef_held = grid.exchange(coef)

    turned, ridged = prepare(place, pieces, width)
    high, low, z = downdate(turned, points, factor, targets)
    z, coef_held = lax.optimization_barrier((z, coef_held))
    coef_held = coef_held.reshape(held, nt)
    t = nt // devices
    z_parts = grid.exchange(z.reshape(devices, t, BLOCK))

    inverse = jnp.zeros((BLOCK, BLOCK), f32)
    middle = BLOCK // TILE // 2
    ridged, inverse = factor_step(ridged, inverse, 0, middle)
    ridged, inverse = factor_step(ridged, inverse, middle, BLOCK // TILE)

    new_columns, new_turned, norm_own = make_columns(inverse, high, low)
    parcel = make_parcel(z_parts, inverse, norm_own)
    every = grid.exchange(parcel).astype(f32)
    norm_new = jnp.sum(every[:, t : t + 3], axis=(0, 1))
    coef_new = (every[:, :t].reshape(nt, BLOCK) / (norm_new + damping)[None, :]).astype(bf16)

    base = targets.astype(f32) - dot(factor, coef_held)
    return new_columns, finish(base, new_turned, coef_new)


def step(grid, *args):
    return on_device(grid, *args)


def solution(mesh):
    spec = P(AXES, None)
    return jax.shard_map(
        functools.partial(step, Grid(mesh)),
        mesh=mesh,
        in_specs=(spec, spec, spec, spec, P()),
        out_specs=(P(None, AXES), spec),
        check_vma=False,
    )
```
